512 devices in a mesh: rep: 128 (over x, y_lo, z), dp: 4 (over y_hi, core).
Axes of the slice: x: 4, y: 4 (y_hi: 2, y_lo: 2; y = y_hi * 2 + y_lo), z: 16, core: 2. Of those that a mesh axis runs over, the one named last changes fastest.
Arguments:
- residual_flow: bfloat16 [1536, 1024], P('dp'), may hold values from -6 to 6
- rooted_input_matrix: bfloat16 [128, 1024, 2048], P('rep', None, 'dp'), may hold values from -6 to 6
- chain_normal_draws: bfloat16 [128, 1024, 2048], P('rep', None, 'dp'), may hold values from -6 to 6
- output_matrix: bfloat16 [2048, 1024], P('dp'), may hold values from -0.125 to 0.125
- chain_heat: float32 [128], P('rep'), may hold values from 0.05 to 1
- matched_chain: int32 [128], P('rep'), may hold values from 0 to 127, as said below
- swap_mask: int32 [128], P('rep'), may hold values from 0 to 1, as said below
Outputs:
- swapped: bfloat16 [128, 1024, 2048], P('rep', None, 'dp')
- chain_gaps: float32 [128, 2, 2048], P('rep', None, 'dp')
The draws below stay inside these ranges and needn't reach their ends.
Inputs may be any that keep to these rules, and one draw needn't show every extreme that they name: Replicas form aligned blocks of four; in each block one of these holds: 4b with 4b + 1 and 4b + 2 with 4b + 3 are mates; only 4b + 1 with 4b + 2; only 4b with 4b + 1; only 4b + 2 with 4b + 3. matched_chain[r] is r's mate, or r where r has none. `swap_mask`: mates carry the same flag; a replica without a mate carries 0; every matched pair of the first block carries 1.
All inputs are finite; a program needn't handle non-finite values.
Results may differ from the reference program's by a relative error of at most 0.014.
Values may be sent and summed in bfloat16 or wider, within the bound.
A program may use at most 64 MiB of HBM per device.

```python
import math
import jax
import jax.numpy as jnp
from jax import lax

D = 1024
FF = 2048
TOK_DEV = 384
TOKENS = 1536
CHAIN_TOTAL = 128


def mating(key):
    rank = jnp.arange(CHAIN_TOTAL, dtype=jnp.int32)
    pattern = jax.random.randint(jax.random.fold_in(key, 17), (CHAIN_TOTAL // 4,), 0, 4)
    local_kind = pattern[rank // 4]
    place = rank % 4
    paired = jnp.bitwise_xor(rank, 1)
    middle = jnp.where(place == 1, rank + 1, jnp.where(place == 2, rank - 1, rank))
    lower_only = jnp.where(place < 2, paired, rank)
    upper_only = jnp.where(place >= 2, paired, rank)
    mate = jnp.where(local_kind == 0, paired, jnp.where(local_kind == 1, middle, jnp.where(local_kind == 2, lower_only, upper_only)))
    coins = jax.random.randint(jax.random.fold_in(key, 29), (CHAIN_TOTAL,), 0, 2)
    lowest = jnp.minimum(mate, rank)
    pair_coin = jnp.where(lowest // 4 == 0, 1, coins[lowest])
    flags = jnp.where(mate != rank, pair_coin, 0)
    return (mate.astype(jnp.int32), flags.astype(jnp.int32))


def draw_matched_chain(key, part):
    return mating(key)[0]


def draw_swap_mask(key, part):
    return mating(key)[1]


def level_of(own_key, dims, cuts, low, high):
    factor_of, own = 1.0, jax.random.fold_in(own_key, 6)
    for axis_at, blocks in cuts:
        heights = jnp.exp(jax.random.uniform(jax.random.fold_in(own, axis_at), (blocks,), jnp.float32, low / len(cuts), high / len(cuts)))
        factor_of = factor_of * jnp.repeat(heights, dims[axis_at] // blocks).reshape([-1 if axis == axis_at else 1 for axis in range(len(dims))])
    return factor_of


def bell_draw(stream_key, extent, scale, bound, pieces=(), kind=jnp.bfloat16):
    result = scale * jax.random.normal(stream_key, extent, jnp.float32)
    if pieces:
        result = result * level_of(stream_key, extent, pieces, -0.22, 0.18)
    return jnp.clip(result, -bound, bound).astype(kind)


def setup_inputs(seed: int = 0) -> dict:
    keys = jax.random.split(jax.random.key(seed), 8)
    residual_flow = bell_draw(keys[0], (TOKENS, D), 1.0, 6.0, ((0, 4),))
    rooted_input_matrix = bell_draw(keys[1], (CHAIN_TOTAL, D, FF), 1.0, 6.0, ((0, 128), (2, 4)))
    chain_normal_draws = bell_draw(keys[2], (CHAIN_TOTAL, D, FF), 1.0, 6.0, ((0, 128), (2, 4)))
    output_matrix = bell_draw(keys[3], (FF, D), FF ** -0.5, 0.125, ((0, 4),))
    chain_heat = jnp.clip(jnp.exp(math.log(1.0) - 2.9957323 * jax.random.uniform(keys[4], (CHAIN_TOTAL,), jnp.float32) ** level_of(keys[4], (CHAIN_TOTAL,), ((0, 128),), -0.2, 0.2)), 0.05, 1.0)
    matched_chain = draw_matched_chain(jax.random.fold_in(keys[7], 71), 0)
    swap_mask = draw_swap_mask(jax.random.fold_in(keys[7], 71), 0)
    return {"residual_flow": residual_flow, "rooted_input_matrix": rooted_input_matrix, "chain_normal_draws": chain_normal_draws, "output_matrix": output_matrix, "chain_heat": chain_heat, "matched_chain": matched_chain, "swap_mask": swap_mask}


drift_stride = 0.5

def normalize(residual_flow):
    values = residual_flow.astype(jnp.float32)
    center = values - lax.optimization_barrier(jnp.mean(values, axis=1, keepdims=True))
    spread = lax.optimization_barrier(jnp.mean(center * center, axis=1, keepdims=True))
    return (center * lax.rsqrt(spread + 1e-05)).astype(jnp.bfloat16)

def gelu_value(values):
    inner = math.sqrt(2.0 / math.pi) * (values + 0.044715 * values * values * values)
    return 0.5 * values * (1.0 + jnp.tanh(inner))

def gelu_slope(values):
    coeff = math.sqrt(2.0 / math.pi)
    inner = coeff * (values + 0.044715 * values * values * values)
    tangent = jnp.tanh(inner)
    return 0.5 * (1.0 + tangent) + 0.5 * values * (1.0 - tangent * tangent) * coeff * (1.0 + 3.0 * 0.044715 * values * values)

def reference(residual_flow, rooted_input_matrix, chain_normal_draws, output_matrix, chain_heat, matched_chain, swap_mask):
    factor = D ** (-0.5)
    normed = normalize(residual_flow)
    blocks = TOKENS // TOK_DEV
    inputs = residual_flow.astype(jnp.float32).reshape(blocks, TOK_DEV, D)

    def lone_chain(items):
        params, noise, temp = items
        preact = jnp.dot(normed, params, preferred_element_type=jnp.float32) * factor
        hidden = gelu_value(preact).astype(jnp.bfloat16)
        output = residual_flow.astype(jnp.float32) + jnp.dot(hidden, output_matrix, preferred_element_type=jnp.float32)
        output = output.reshape(blocks, TOK_DEV, D)
        errors = jnp.concatenate([output[:, :-1] - inputs[:, 1:], jnp.zeros((blocks, 1, D), jnp.float32)], axis=1)
        errors = errors.reshape(TOKENS, D).astype(jnp.bfloat16)
        hidden_grad = jnp.dot(errors, output_matrix.T, preferred_element_type=jnp.float32)
        preact_grad = (hidden_grad * gelu_slope(preact)).astype(jnp.bfloat16)
        partial_value = jnp.einsum('ktd,ktf->kdf', normed.reshape(blocks, TOK_DEV, D).astype(jnp.float32), preact_grad.reshape(blocks, TOK_DEV, FF).astype(jnp.float32)) * factor
        gradient = lax.optimization_barrier(jnp.sum(partial_value.astype(jnp.bfloat16).astype(jnp.float32), axis=0))
        current = params.astype(jnp.float32)
        moved = current - drift_stride * (gradient + current) + jnp.sqrt(2.0 * drift_stride * temp) * noise.astype(jnp.float32)
        return moved.astype(jnp.bfloat16)
    refreshed_input_matrix = lax.map(lone_chain, (rooted_input_matrix, chain_normal_draws, chain_heat))

    def gap_of(index):
        own = refreshed_input_matrix[index].astype(jnp.float32)
        below = refreshed_input_matrix[(index - 1) % CHAIN_TOTAL].astype(jnp.float32)
        above = refreshed_input_matrix[(index + 1) % CHAIN_TOTAL].astype(jnp.float32)
        lower_gap = lax.optimization_barrier(jnp.mean((own - below) * (own - below), axis=0))
        upper_gap = lax.optimization_barrier(jnp.mean((own - above) * (own - above), axis=0))
        return jnp.stack([lower_gap, upper_gap], axis=0)
    chain_gaps = lax.map(gap_of, jnp.arange(CHAIN_TOTAL, dtype=jnp.int32))
    taken = (swap_mask == 1)[:, None, None]
    swapped = jnp.where(taken, refreshed_input_matrix[matched_chain.astype(jnp.int32)], refreshed_input_matrix)
    return (swapped, chain_gaps)
```

```python
import math

import jax
import jax.numpy as jnp
from jax import lax
from jax.sharding import PartitionSpec as P

drift_stride = 0.5


def shifted(value, axis, steps):
    count = lax.axis_size(axis)
    pairs = [(source, (source + steps) % count) for source in range(count)]
    return lax.ppermute(value, axis, pairs)


def normalize(residual_flow):
    values = residual_flow.astype(jnp.float32)
    center = values - jnp.mean(values, axis=1, keepdims=True)
    spread = jnp.mean(center * center, axis=1, keepdims=True)
    return (center * lax.rsqrt(spread + 1e-05)).astype(jnp.bfloat16)


def gelu_value(values):
    inner = math.sqrt(2.0 / math.pi) * (values + 0.044715 * values * values * values)
    return 0.5 * values * (1.0 + jnp.tanh(inner))


def gelu_slope(values):
    coeff = math.sqrt(2.0 / math.pi)
    inner = coeff * (values + 0.044715 * values * values * values)
    tangent = jnp.tanh(inner)
    return 0.5 * (1.0 + tangent) + 0.5 * values * (1.0 - tangent * tangent) * coeff * (
        1.0 + 3.0 * 0.044715 * values * values
    )


def next_errors(output, residual_flow):
    width = residual_flow.shape[1]
    ahead = output[:-1] - residual_flow[1:].astype(jnp.float32)
    return jnp.concatenate([ahead, jnp.zeros((1, width), jnp.float32)], axis=0).astype(jnp.bfloat16)


def against_rows(errors, weight):
    return lax.dot_general(
        errors, weight, (((1,), (1,)), ((), ())), preferred_element_type=jnp.float32
    )


def body(
    residual_flow,
    rooted_input_matrix,
    chain_normal_draws,
    output_matrix,
    chain_heat,
    matched_chain,
    swap_mask,
):
    width = rooted_input_matrix.shape[1]
    factor = width ** (-0.5)
    params = rooted_input_matrix[0]
    normed = lax.all_gather(normalize(residual_flow), "dp", axis=0, tiled=True)
    preact = jnp.dot(normed, params, preferred_element_type=jnp.float32) * factor
    hidden = gelu_value(preact).astype(jnp.bfloat16)
    part = jnp.dot(hidden, output_matrix, preferred_element_type=jnp.float32)
    own = residual_flow.astype(jnp.float32) + lax.psum_scatter(
        part.astype(jnp.bfloat16), "dp", scatter_dimension=0, tiled=True
    ).astype(jnp.float32)
    errors = lax.all_gather(next_errors(own, residual_flow), "dp", axis=0, tiled=True)
    hidden_grad = against_rows(errors, output_matrix)
    preact_grad = (hidden_grad * gelu_slope(preact)).astype(jnp.bfloat16)
    gradient = (
        lax.dot_general(
            normed, preact_grad, (((0,), (0,)), ((), ())), preferred_element_type=jnp.float32
        )
        * factor
    )
    current = params.astype(jnp.float32)
    moved = (
        current
        - drift_stride * (gradient + current)
        + jnp.sqrt(2.0 * drift_stride * chain_heat[0]) * chain_normal_draws[0].astype(jnp.float32)
    )
    refreshed_input_matrix = moved.astype(jnp.bfloat16)
    own_rank = lax.axis_index("rep")
    mate = matched_chain[0]
    taken = swap_mask[0] == 1
    below = shifted(refreshed_input_matrix, "rep", 1)
    above = shifted(refreshed_input_matrix, "rep", -1)
    result = jnp.where(
        taken & (mate == own_rank - 1),
        below,
        jnp.where(taken & (mate == own_rank + 1), above, refreshed_input_matrix),
    )
    own_values = refreshed_input_matrix.astype(jnp.float32)
    lower_diff = own_values - below.astype(jnp.float32)
    upper_diff = own_values - above.astype(jnp.float32)
    chain_gaps = jnp.stack(
        [jnp.mean(lower_diff * lower_diff, axis=0), jnp.mean(upper_diff * upper_diff, axis=0)],
        axis=0,
    )
    return (result[None], chain_gaps[None])


def solution(mesh):
    placed = (
        P("dp", None),
        P("rep", None, "dp"),
        P("rep", None, "dp"),
        P("dp", None),
        P("rep"),
        P("rep"),
        P("rep"),
    )
    return jax.shard_map(
        body,
        mesh=mesh,
        in_specs=placed,
        out_specs=(P("rep", None, "dp"), P("rep", None, "dp")),
        check_vma=False,
    )
```

```python
import functools
import math

import jax
import jax.numpy as jnp
from jax import lax
from jax.experimental import pallas as pl
from jax.experimental.pallas import tpu as pltpu
from jax.sharding import PartitionSpec as P

MESH = pl.DeviceIdType.MESH
drift_stride = 0.5
TILE = 128
CHUNK = 256


def place():
    rep = lax.axis_index("rep")
    dp = lax.axis_index("dp")
    return rep, rep // 32, (rep // 16) % 2, rep % 16, dp // 2, dp % 2


def peers():
    rep, x, y_lo, z, y_hi, core = place()
    dp = y_hi * 2 + core

    def at(x, y_lo, y_hi, core):
        return ((x * 2 + y_lo) * 16 + z, y_hi * 2 + core)

    return {
        "sibling": at(x, y_lo, y_hi, 1 - core),
        "partner": at(x, y_lo, 1 - y_hi, core),
        "across": at(x, 1 - y_lo, 1 - y_hi, core),
        "x1": at((x + 1) % 4, y_lo, y_hi, core),
        "x2": at((x + 2) % 4, y_lo, y_hi, core),
        "x3": at((x + 3) % 4, y_lo, y_hi, core),
        "up": ((rep + 1) % 128, dp),
        "down": ((rep + 127) % 128, dp),
    }


def kernel(
    res_hbm,
    par_hbm,
    noise_hbm,
    down_hbm,
    heat,
    mate,
    mask,
    out_ref,
    gap_ref,
    res,
    par,
    noise,
    down,
    nrm,
    flip,
    flip_sib,
    slope,
    base,
    op_send,
    op_recv,
    hid,
    pg_send,
    pg_own,
    pg_sib,
    acc,
    rest,
    fresh,
    near,
    load_sem,
    swap_s,
    swap_r,
    quart_s,
    quart_r,
    spread_s,
    spread_r,
    flip_s,
    flip_r,
    op_s,
    op_r,
    pg_s,
    pg_r,
    z_s,
    z_r,
):
    factor = 1024 ** (-0.5)
    coeff = math.sqrt(2.0 / math.pi)
    rank, x = place()[:2]
    peer = peers()

    def remote(src, dst, send, recv, who):
        return pltpu.make_async_remote_copy(
            src_ref=src,
            dst_ref=dst,
            send_sem=send,
            recv_sem=recv,
            device_id=peer[who],
            device_id_type=MESH,
        )

    loads = [
        pltpu.make_async_copy(res_hbm, res.at[0], load_sem.at[0]),
        pltpu.make_async_copy(par_hbm.at[0], par.at[0], load_sem.at[1]),
        pltpu.make_async_copy(down_hbm, down.at[0], load_sem.at[2]),
        pltpu.make_async_copy(noise_hbm.at[0], noise, load_sem.at[3]),
    ]
    for copy in loads:
        copy.start()

    barrier = pltpu.get_barrier_semaphore()
    for who in peer:
        pl.semaphore_signal(barrier, inc=1, device_id=peer[who], device_id_type=MESH)
    pl.semaphore_wait(barrier, len(peer))

    quarter = pl.ds(pl.multiple_of(x * 96, 96), 96)
    loads[0].wait()
    quart = remote(res.at[0, quarter], res.at[1, quarter], quart_s, quart_r, "across")
    quart.start()
    loads[1].wait()
    swap_par = remote(par.at[0], par.at[1], swap_s.at[0], swap_r.at[0], "sibling")
    swap_par.start()
    loads[2].wait()
    swap_down = remote(down.at[0], down.at[1], swap_s.at[1], swap_r.at[1], "sibling")
    swap_down.start()

    def flip_copy(j):
        return remote(flip.at[j], flip_sib.at[j], flip_s.at[j], flip_r.at[j], "sibling")

    def op_copy(j):
        return remote(
            op_send.at[j], op_recv.at[(j + 3) % 6], op_s.at[j], op_r.at[(j + 3) % 6], "partner"
        )

    def pg_copy(j):
        return remote(pg_send.at[j], pg_sib.at[j], pg_s.at[j], pg_r.at[j], "sibling")

    def prepare(seq):
        def one(k, _):
            rows = pl.ds(pl.multiple_of(k * TILE, TILE), TILE)
            values = res[seq, rows, :].astype(jnp.float32)
            center = values - jnp.mean(values, axis=1, keepdims=True)
            spread = jnp.mean(center * center, axis=1, keepdims=True)
            nrm[seq * 3 + k] = (center * lax.rsqrt(spread + 1e-05)).astype(jnp.bfloat16)
            return 0

        lax.fori_loop(0, 3, one, 0)

    def step_ahead(seq):
        for c in range(4):
            cols = slice(c * CHUNK, (c + 1) * CHUNK)
            values = res[seq, :, cols].astype(jnp.float32)
            ahead = values - pltpu.roll(values, 383, 0)
            for k in range(3):
                base[seq * 3 + k, :, cols] = ahead[k * TILE : (k + 1) * TILE]

    def forward(j, _):
        rows = nrm[j]
        for c in range(4):
            cols = slice((c % 2) * CHUNK, (c % 2 + 1) * CHUNK)
            wide = slice(c * CHUNK, (c + 1) * CHUNK)
            v = jnp.dot(rows, par[c // 2, :, cols], preferred_element_type=jnp.float32) * factor
            square = v * v
            tangent = jnp.tanh(coeff * v * (1.0 + 0.044715 * square))
            half = 0.5 * (1.0 + tangent)
            hid[:, wide] = (v * half).astype(jnp.bfloat16)
            slope[j, :, wide] = half + 0.5 * coeff * v * (1.0 - tangent * tangent) * (
                1.0 + 3.0 * 0.044715 * square
            )
        for c in range(4):
            wide = slice(c * CHUNK, (c + 1) * CHUNK)
            part = jnp.dot(
                hid[:, :512], down[0, :, wide], preferred_element_type=jnp.float32
            ) + jnp.dot(hid[:, 512:], down[1, :, wide], preferred_element_type=jnp.float32)
            base[j, :, wide] += part
            op_send[j, :, wide] = part.astype(jnp.bfloat16)
        op_copy(j).start()
        return 0

    def turn(j, _):
        flip[j] = nrm[j].T
        flip_copy(j).start()
        return 0

    prepare(0)
    step_ahead(0)
    swap_par.wait_recv()
    swap_down.wait_recv()
    quart.wait_recv()
    spreads = [
        remote(
            res.at[1, quarter], res.at[1, quarter], spread_s.at[k - 1], spread_r.at[k - 1], f"x{k}"
        )
        for k in (1, 2, 3)
    ]
    for copy in spreads:
        copy.start()
    lax.fori_loop(0, 3, forward, 0)
    lax.fori_loop(0, 3, turn, 0)

    loads[3].wait()
    heat_root = jnp.sqrt(jnp.full((1, 512), 2.0 * drift_stride * heat[0], jnp.float32))

    def keep(k, _):
        rows = pl.ds(pl.multiple_of(k * TILE, TILE), TILE)
        current = par[0, rows, :].astype(jnp.float32)
        rest[rows, :] = (
            current - drift_stride * current + heat_root * noise[rows, :].astype(jnp.float32)
        )
        acc[rows, :] = jnp.zeros((TILE, 512), jnp.float32)
        return 0

    lax.fori_loop(0, 8, keep, 0)

    for copy in spreads:
        copy.wait_recv()
    prepare(1)
    step_ahead(1)
    lax.fori_loop(3, 6, forward, 0)
    lax.fori_loop(3, 6, turn, 0)

    def backward(j):
        op_copy((j + 3) % 6).wait_recv()
        keepers = lax.broadcasted_iota(jnp.int32, (TILE, 1), 0) + (j % 3) * TILE < 383
        errors = jnp.where(keepers, base[j] + op_recv[j].astype(jnp.float32), 0.0).astype(
            jnp.bfloat16
        )
        for side in (1, 0):
            grad = lax.dot_general(
                errors, down[side], (((1,), (1,)), ((), ())), preferred_element_type=jnp.float32
            )
            grad = (grad * slope[j, :, side * 512 : side * 512 + 512]).astype(jnp.bfloat16)
            if side == 1:
                pg_send[j] = grad
                pg_copy(j).start()
            else:
                pg_own[j] = grad

    def arrive(j):
        pg_copy(j).wait_recv()
        flip_copy(j).wait_recv()

    def product(j, k):
        rows = pl.ds(pl.multiple_of(k * CHUNK, CHUNK), CHUNK)
        left = jnp.concatenate([flip[j, rows, :], flip_sib[j, rows, :]], axis=1)
        right = jnp.concatenate([pg_own[j], pg_sib[j]], axis=0)
        return jnp.dot(left, right, preferred_element_type=jnp.float32)

    def gather(j):
        arrive(j)

        def one(k, _):
            rows = pl.ds(pl.multiple_of(k * CHUNK, CHUNK), CHUNK)
            acc[rows, :] += product(j, k)
            return 0

        lax.fori_loop(0, 4, one, 0)

    backward(3)

    def steps(i, _):
        backward((i + 3) % 6)
        gather((i + 2) % 6)
        return 0

    lax.fori_loop(1, 6, steps, 0)

    def z_copy(side, k):
        rows = pl.ds(k * CHUNK, CHUNK)
        return remote(
            fresh.at[rows],
            near.at[side, rows],
            z_s.at[side, k],
            z_r.at[side, k],
            ("up", "down")[side],
        )

    arrive(2)
    for k in range(4):
        rows = slice(k * CHUNK, (k + 1) * CHUNK)
        total = acc[rows, :] + product(2, k)
        fresh[rows, :] = (rest[rows, :] - (drift_stride * factor) * total).astype(jnp.bfloat16)
        z_copy(0, k).start()
        z_copy(1, k).start()

    taken = jnp.full((1, 512), mask[0], jnp.int32) == 1
    mates = jnp.full((1, 512), mate[0], jnp.int32)
    from_below = taken & (mates == rank - 1)
    from_above = taken & (mates == rank + 1)
    lower = jnp.zeros((1, 512), jnp.float32)
    upper = jnp.zeros((1, 512), jnp.float32)
    for k in range(4):
        rows = slice(k * CHUNK, (k + 1) * CHUNK)
        z_copy(0, k).wait_recv()
        z_copy(1, k).wait_recv()
        own = fresh[rows, :].astype(jnp.float32)
        below = near[0, rows, :].astype(jnp.float32)
        above = near[1, rows, :].astype(jnp.float32)
        lower += jnp.sum((own - below) * (own - below), axis=0, keepdims=True)
        upper += jnp.sum((own - above) * (own - above), axis=0, keepdims=True)
        out_ref[0, rows, :] = jnp.where(
            from_below, below, jnp.where(from_above, above, own)
        ).astype(jnp.bfloat16)
    gap_ref[0, 0:1, :] = lower * (1.0 / 1024.0)
    gap_ref[0, 1:2, :] = upper * (1.0 / 1024.0)

    quart.wait_send()
    swap_par.wait_send()
    swap_down.wait_send()
    for copy in spreads:
        copy.wait_send()

    def finish(j, _):
        flip_copy(j).wait_send()
        op_copy(j).wait_send()
        pg_copy(j).wait_send()
        return 0

    lax.fori_loop(0, 6, finish, 0)
    for k in range(4):
        z_copy(0, k).wait_send()
        z_copy(1, k).wait_send()


def body(residual_flow, params, noise, down, heat, mate, mask):
    any_spec = pl.BlockSpec(memory_space=pl.ANY)
    scalar = pl.BlockSpec(memory_space=pltpu.SMEM)
    vmem = pl.BlockSpec(memory_space=pltpu.VMEM)
    bf16, f32 = jnp.bfloat16, jnp.float32
    dma = pltpu.SemaphoreType.DMA
    return pl.pallas_call(
        kernel,
        out_shape=(
            jax.ShapeDtypeStruct((1, 1024, 512), bf16),
            jax.ShapeDtypeStruct((1, 2, 512), f32),
        ),
        in_specs=[any_spec] * 4 + [scalar] * 3,
        out_specs=(vmem, vmem),
        scratch_shapes=[
            pltpu.VMEM((2, 384, 1024), bf16),
            pltpu.VMEM((2, 1024, 512), bf16),
            pltpu.VMEM((1024, 512), bf16),
            pltpu.VMEM((2, 512, 1024), bf16),
            pltpu.VMEM((6, TILE, 1024), bf16),
            pltpu.VMEM((6, 1024, TILE), bf16),
            pltpu.VMEM((6, 1024, TILE), bf16),
            pltpu.VMEM((6, TILE, 1024), f32),
            pltpu.VMEM((6, TILE, 1024), f32),
            pltpu.VMEM((6, TILE, 1024), bf16),
            pltpu.VMEM((6, TILE, 1024), bf16),
            pltpu.VMEM((TILE, 1024), bf16),
            pltpu.VMEM((6, TILE, 512), bf16),
            pltpu.VMEM((6, TILE, 512), bf16),
            pltpu.VMEM((6, TILE, 512), bf16),
            pltpu.VMEM((1024, 512), f32),
            pltpu.VMEM((1024, 512), f32),
            pltpu.VMEM((1024, 512), bf16),
            pltpu.VMEM((2, 1024, 512), bf16),
            dma((4,)),
            dma((2,)),
            dma((2,)),
            dma(()),
            dma(()),
            dma((3,)),
            dma((3,)),
            dma((6,)),
            dma((6,)),
            dma((6,)),
            dma((6,)),
            dma((6,)),
            dma((6,)),
            dma((2, 4)),
            dma((2, 4)),
        ],
        compiler_params=pltpu.CompilerParams(
            collective_id=0, has_side_effects=True, vmem_limit_bytes=56 << 20
        ),
        name="langevin_step",
    )(residual_flow, params, noise, down, heat, mate, mask)


def solution(mesh):
    placed = (
        P("dp", None),
        P("rep", None, "dp"),
        P("rep", None, "dp"),
        P("dp", None),
        P("rep"),
        P("rep"),
        P("rep"),
    )
    return jax.shard_map(
        body,
        mesh=mesh,
        in_specs=placed,
        out_specs=(P("rep", None, "dp"), P("rep", None, "dp")),
        check_vma=False,
    )
```

```python
import functools
import math

import jax
import jax.numpy as jnp
from jax import lax
from jax.experimental import pallas as pl
from jax.experimental.pallas import tpu as pltpu
from jax.sharding import PartitionSpec as P

MESH = pl.DeviceIdType.MESH
drift_stride = 0.5
TILE = 128
CHUNK = 256
SHARE = 256
KEEP = 512 - SHARE


def place():
    rep = lax.axis_index("rep")
    dp = lax.axis_index("dp")
    return rep, rep // 32, (rep // 16) % 2, rep % 16, dp // 2, dp % 2


def peers():
    rep, x, y_lo, z, y_hi, core = place()
    dp = y_hi * 2 + core

    def at(x, y_lo, y_hi, core):
        return ((x * 2 + y_lo) * 16 + z, y_hi * 2 + core)

    return {
        "sibling": at(x, y_lo, y_hi, 1 - core),
        "partner": at(x, y_lo, 1 - y_hi, core),
        "across": at(x, 1 - y_lo, 1 - y_hi, core),
        "x1": at((x + 1) % 4, y_lo, y_hi, core),
        "x2": at((x + 2) % 4, y_lo, y_hi, core),
        "x3": at((x + 3) % 4, y_lo, y_hi, core),
        "up": ((rep + 1) % 128, dp),
        "down": ((rep + 127) % 128, dp),
    }


def kernel(
    res_hbm,
    par_hbm,
    noise_hbm,
    down_hbm,
    heat,
    mate,
    mask,
    out_ref,
    gap_ref,
    res,
    par,
    noise,
    down,
    nrm,
    flip,
    flip_sib,
    slope,
    base,
    op_send,
    op_recv,
    hid,
    pg_send_b,
    pg_send_a,
    pg_b,
    pg_a,
    acc,
    rest,
    fresh_b,
    fresh_a,
    near_b,
    near_a,
    rest_send,
    rest_near,
    pg_near,
    acc_near,
    gap_sum,
    gap_recv,
    load_sem,
    swap_s,
    swap_r,
    quart_s,
    quart_r,
    spread_s,
    spread_r,
    flip_s,
    flip_r,
    op_s,
    op_r,
    pg_s,
    pg_r,
    w_s,
    w_r,
    zp_s,
    zp_r,
    za_s,
    za_r,
    zb_s,
    zb_r,
    gx_s,
    gx_r,
):
    factor = 1024 ** (-0.5)
    coeff = math.sqrt(2.0 / math.pi)
    rank, x = place()[:2]
    peer = peers()
    spot = rank % 4
    mixes = (spot != 0, spot != 3)
    sends = (spot != 3, spot != 0)
    ways = ("up", "down")

    def remote(src, dst, send, recv, who):
        return pltpu.make_async_remote_copy(
            src_ref=src,
            dst_ref=dst,
            send_sem=send,
            recv_sem=recv,
            device_id=peer[who],
            device_id_type=MESH,
        )

    loads = [
        pltpu.make_async_copy(res_hbm, res.at[0], load_sem.at[0]),
        pltpu.make_async_copy(par_hbm.at[0], par.at[0], load_sem.at[1]),
        pltpu.make_async_copy(down_hbm, down.at[0], load_sem.at[2]),
        pltpu.make_async_copy(noise_hbm.at[0], noise, load_sem.at[3]),
    ]
    for copy in loads:
        copy.start()

    barrier = pltpu.get_barrier_semaphore()
    for who in peer:
        pl.semaphore_signal(barrier, inc=1, device_id=peer[who], device_id_type=MESH)
    pl.semaphore_wait(barrier, len(peer))

    quarter = pl.ds(pl.multiple_of(x * 96, 96), 96)
    loads[0].wait()
    quart = remote(res.at[0, quarter], res.at[1, quarter], quart_s, quart_r, "across")
    quart.start()
    loads[1].wait()
    swap_par = remote(par.at[0], par.at[1], swap_s.at[0], swap_r.at[0], "sibling")
    swap_par.start()
    loads[2].wait()
    swap_down = remote(down.at[0], down.at[1], swap_s.at[1], swap_r.at[1], "sibling")
    swap_down.start()

    def flip_copy(j):
        return remote(flip.at[j], flip_sib.at[j], flip_s.at[j], flip_r.at[j], "sibling")

    def op_copy(j):
        return remote(
            op_send.at[j], op_recv.at[(j + 3) % 6], op_s.at[j], op_r.at[(j + 3) % 6], "partner"
        )

    def pg_copies(j):
        low = pl.ds(TILE, TILE)
        return [
            remote(pg_send_b.at[j], pg_b.at[j, low], pg_s.at[0, j], pg_r.at[0, j], "sibling"),
            remote(pg_send_a.at[j], pg_a.at[j, low], pg_s.at[1, j], pg_r.at[1, j], "sibling"),
        ]

    def w_copy(side):
        return remote(rest_send, rest_near.at[side], w_s.at[side], w_r.at[side], ways[side])

    def zp_copy(side, j):
        return remote(
            pg_b.at[j], pg_near.at[side, j], zp_s.at[side, j], zp_r.at[side, j], ways[side]
        )

    def za_copy(side, k):
        rows = pl.ds(k * CHUNK, CHUNK)
        return remote(
            fresh_a.at[rows], near_a.at[side, rows], za_s.at[side, k], za_r.at[side, k], ways[side]
        )

    def zb_copy(side, k):
        rows = pl.ds(k * CHUNK, CHUNK)
        return remote(
            fresh_b.at[rows], near_b.at[side, rows], zb_s.at[side, k], zb_r.at[side, k], ways[side]
        )

    def gx_copy(side):
        return remote(
            gap_sum.at[1 - side], gap_recv.at[side], gx_s.at[side], gx_r.at[side], ways[side]
        )

    def halves(side, k):
        return (k < 2) == (side == 0)

    def prepare(seq):
        def one(k, _):
            rows = pl.ds(pl.multiple_of(k * TILE, TILE), TILE)
            values = res[seq, rows, :].astype(jnp.float32)
            center = values - jnp.mean(values, axis=1, keepdims=True)
            spread = jnp.mean(center * center, axis=1, keepdims=True)
            nrm[seq * 3 + k] = (center * lax.rsqrt(spread + 1e-05)).astype(jnp.bfloat16)
            return 0

        lax.fori_loop(0, 3, one, 0)

    def step_ahead(seq):
        for c in range(4):
            cols = slice(c * CHUNK, (c + 1) * CHUNK)
            values = res[seq, :, cols].astype(jnp.float32)
            ahead = values - pltpu.roll(values, 383, 0)
            for k in range(3):
                base[seq * 3 + k, :, cols] = ahead[k * TILE : (k + 1) * TILE]

    def forward(j, _):
        rows = nrm[j]
        for c in range(4):
            cols = slice((c % 2) * CHUNK, (c % 2 + 1) * CHUNK)
            wide = slice(c * CHUNK, (c + 1) * CHUNK)
            v = jnp.dot(rows, par[c // 2, :, cols], preferred_element_type=jnp.float32) * factor
            square = v * v
            tangent = jnp.tanh(coeff * v * (1.0 + 0.044715 * square))
            half = 0.5 * (1.0 + tangent)
            hid[:, wide] = (v * half).astype(jnp.bfloat16)
            slope[j, :, wide] = half + 0.5 * coeff * v * (1.0 - tangent * tangent) * (
                1.0 + 3.0 * 0.044715 * square
            )
        for c in range(4):
            wide = slice(c * CHUNK, (c + 1) * CHUNK)
            part = jnp.dot(
                hid[:, :512], down[0, :, wide], preferred_element_type=jnp.float32
            ) + jnp.dot(hid[:, 512:], down[1, :, wide], preferred_element_type=jnp.float32)
            base[j, :, wide] += part
            op_send[j, :, wide] = part.astype(jnp.bfloat16)
        op_copy(j).start()
        return 0

    def turn(j, _):
        flip[j] = nrm[j].T
        flip_copy(j).start()
        return 0

    loads[3].wait()
    heat_root = jnp.sqrt(jnp.full((1, 512), 2.0 * drift_stride * heat[0], jnp.float32))

    def keep(k, _):
        rows = pl.ds(pl.multiple_of(k * TILE, TILE), TILE)
        current = par[0, rows, :].astype(jnp.float32)
        still = current - drift_stride * current + heat_root * noise[rows, :].astype(jnp.float32)
        rest[rows, :] = still
        rest_send[rows, :] = still[:, :SHARE].astype(jnp.bfloat16)
        acc[rows, :] = jnp.zeros((TILE, 512), jnp.float32)
        for side in range(2):
            acc_near[side, rows, :] = jnp.zeros((TILE, SHARE), jnp.float32)
        return 0

    prepare(0)
    lax.fori_loop(0, 8, keep, 0)
    for side in range(2):
        pl.when(sends[side])(w_copy(side).start)
    step_ahead(0)
    lax.fori_loop(0, 3, turn, 0)
    swap_par.wait_recv()
    swap_down.wait_recv()
    forward(0, 0)
    quart.wait_recv()
    spreads = [
        remote(
            res.at[1, quarter], res.at[1, quarter], spread_s.at[k - 1], spread_r.at[k - 1], f"x{k}"
        )
        for k in (1, 2, 3)
    ]
    for copy in spreads:
        copy.start()
    lax.fori_loop(1, 3, forward, 0)

    for copy in spreads:
        copy.wait_recv()
    prepare(1)
    step_ahead(1)
    lax.fori_loop(3, 6, forward, 0)
    lax.fori_loop(3, 6, turn, 0)

    def backward(j):
        op_copy((j + 3) % 6).wait_recv()
        keepers = lax.broadcasted_iota(jnp.int32, (TILE, 1), 0) + (j % 3) * TILE < 383
        errors = jnp.where(keepers, base[j] + op_recv[j].astype(jnp.float32), 0.0).astype(
            jnp.bfloat16
        )
        for side in (1, 0):
            grad = lax.dot_general(
                errors, down[side], (((1,), (1,)), ((), ())), preferred_element_type=jnp.float32
            )
            grad = (grad * slope[j, :, side * 512 : side * 512 + 512]).astype(jnp.bfloat16)
            if side == 1:
                pg_send_b[j] = grad[:, :SHARE]
                pg_send_a[j] = grad[:, SHARE:]
                for copy in pg_copies(j):
                    copy.start()
            else:
                pg_b[j, :TILE] = grad[:, :SHARE]
                pg_a[j, :TILE] = grad[:, SHARE:]

    def arrive(j):
        for copy in pg_copies(j):
            copy.wait_recv()
        for side in range(2):
            pl.when(sends[side])(zp_copy(side, j).start)
        flip_copy(j).wait_recv()

    def left(j, k):
        rows = pl.ds(pl.multiple_of(k * CHUNK, CHUNK), CHUNK)
        return jnp.concatenate([flip[j, rows, :], flip_sib[j, rows, :]], axis=1)

    def product(j, k):
        right = jnp.concatenate([pg_b[j], pg_a[j]], axis=1)
        return jnp.dot(left(j, k), right, preferred_element_type=jnp.float32)

    def gather_near(j):
        for side in range(2):

            @pl.when(mixes[side])
            def _():
                zp_copy(side, j).wait_recv()

                def one(k, _):
                    rows = pl.ds(pl.multiple_of(k * CHUNK, CHUNK), CHUNK)
                    acc_near[side, rows, :] += jnp.dot(
                        left(j, k), pg_near[side, j], preferred_element_type=jnp.float32
                    )
                    return 0

                lax.fori_loop(0, 4, one, 0)

    def gather(j):
        arrive(j)

        def one(k, _):
            rows = pl.ds(pl.multiple_of(k * CHUNK, CHUNK), CHUNK)
            acc[rows, :] += product(j, k)
            return 0

        lax.fori_loop(0, 4, one, 0)

    backward(3)
    backward(4)
    gather(3)

    def steps(i, _):
        backward((i + 3) % 6)
        gather((i + 2) % 6)
        gather_near((i + 1) % 6)
        return 0

    lax.fori_loop(2, 6, steps, 0)

    arrive(2)
    for k in range(4):
        rows = slice(k * CHUNK, (k + 1) * CHUNK)
        total = acc[rows, :] + product(2, k)
        moved = (rest[rows, :] - (drift_stride * factor) * total).astype(jnp.bfloat16)
        fresh_b[rows, :] = moved[:, :SHARE]
        fresh_a[rows, :] = moved[:, SHARE:]
        for side in range(2):
            pl.when(sends[side])(za_copy(side, k).start)
            if halves(side, k):

                @pl.when(jnp.logical_not(sends[side]))
                def _():
                    za_copy(side, k).start()
                    zb_copy(side, k).start()

    gather_near(1)
    gather_near(2)
    for side in range(2):

        @pl.when(mixes[side])
        def _():
            w_copy(side).wait_recv()

            def one(k, _):
                rows = pl.ds(pl.multiple_of(k * CHUNK, CHUNK), CHUNK)
                near_b[side, rows, :] = (
                    rest_near[side, rows, :].astype(jnp.float32)
                    - (drift_stride * factor) * acc_near[side, rows, :]
                ).astype(jnp.bfloat16)
                return 0

            lax.fori_loop(0, 4, one, 0)

    taken = jnp.full((1, 512), mask[0], jnp.int32) == 1
    mates = jnp.full((1, 512), mate[0], jnp.int32)
    picks = (taken & (mates == rank - 1), taken & (mates == rank + 1))
    gap_sum[...] = jnp.zeros((2, 8, 512), jnp.float32)
    pairs = ((0, SHARE, fresh_b, near_b), (SHARE, 512, fresh_a, near_a))
    for k in range(4):
        rows = slice(k * CHUNK, (k + 1) * CHUNK)

        def add_gap(side):
            for first, last, own_ref, near_ref in pairs:
                gap = own_ref[rows, :].astype(jnp.float32) - near_ref[side, rows, :].astype(
                    jnp.float32
                )
                gap_sum[side, :, first:last] += jnp.sum(
                    (gap * gap).reshape(CHUNK // 8, 8, last - first), axis=0
                )

        for side in range(2):

            @pl.when(mixes[side])
            def _():
                za_copy(side, k).wait_recv()
                add_gap(side)

            if halves(side, k):

                @pl.when(jnp.logical_not(mixes[side]))
                def _():
                    za_copy(side, k).wait_recv()
                    zb_copy(side, k).wait_recv()
                    add_gap(side)

        for side in range(2):
            if k == (1, 3)[side]:
                pl.when(jnp.logical_not(mixes[side]))(gx_copy(1 - side).start)
        for first, last, own_ref, near_ref in pairs:
            out_ref[0, rows, first:last] = jnp.where(
                picks[0][:, first:last],
                near_ref[0, rows, :],
                jnp.where(picks[1][:, first:last], near_ref[1, rows, :], own_ref[rows, :]),
            )

    for side in range(2):

        @pl.when(jnp.logical_not(mixes[side]))
        def _():
            gx_copy(side).wait_recv()
            gap_recv[side] += gap_sum[side]
            gap_ref[0, side : side + 1, :] = jnp.sum(gap_recv[side], axis=0, keepdims=True) * (
                1.0 / 1024.0
            )

        @pl.when(mixes[side])
        def _():
            gap_ref[0, side : side + 1, :] = jnp.sum(gap_sum[side], axis=0, keepdims=True) * (
                1.0 / 1024.0
            )

    quart.wait_send()
    swap_par.wait_send()
    swap_down.wait_send()
    for copy in spreads:
        copy.wait_send()

    def finish(j, _):
        flip_copy(j).wait_send()
        op_copy(j).wait_send()
        for copy in pg_copies(j):
            copy.wait_send()
        for side in range(2):
            pl.when(sends[side])(zp_copy(side, j).wait_send)
        return 0

    lax.fori_loop(0, 6, finish, 0)
    for side in range(2):

        @pl.when(sends[side])
        def _():
            w_copy(side).wait_send()
            for k in range(4):
                za_copy(side, k).wait_send()

        @pl.when(jnp.logical_not(sends[side]))
        def _():
            gx_copy(side).wait_send()
            for k in range(4):
                if halves(side, k):
                    za_copy(side, k).wait_send()
                    zb_copy(side, k).wait_send()


def body(residual_flow, params, noise, down, heat, mate, mask):
    any_spec = pl.BlockSpec(memory_space=pl.ANY)
    scalar = pl.BlockSpec(memory_space=pltpu.SMEM)
    vmem = pl.BlockSpec(memory_space=pltpu.VMEM)
    bf16, f32 = jnp.bfloat16, jnp.float32
    dma = pltpu.SemaphoreType.DMA
    return pl.pallas_call(
        kernel,
        out_shape=(
            jax.ShapeDtypeStruct((1, 1024, 512), bf16),
            jax.ShapeDtypeStruct((1, 2, 512), f32),
        ),
        in_specs=[any_spec] * 4 + [scalar] * 3,
        out_specs=(vmem, vmem),
        scratch_shapes=[
            pltpu.VMEM((2, 384, 1024), bf16),
            pltpu.VMEM((2, 1024, 512), bf16),
            pltpu.VMEM((1024, 512), bf16),
            pltpu.VMEM((2, 512, 1024), bf16),
            pltpu.VMEM((6, TILE, 1024), bf16),
            pltpu.VMEM((6, 1024, TILE), bf16),
            pltpu.VMEM((6, 1024, TILE), bf16),
            pltpu.VMEM((6, TILE, 1024), f32),
            pltpu.VMEM((6, TILE, 1024), f32),
            pltpu.VMEM((6, TILE, 1024), bf16),
            pltpu.VMEM((6, TILE, 1024), bf16),
            pltpu.VMEM((TILE, 1024), bf16),
            pltpu.VMEM((6, TILE, SHARE), bf16),
            pltpu.VMEM((6, TILE, KEEP), bf16),
            pltpu.VMEM((6, 2 * TILE, SHARE), bf16),
            pltpu.VMEM((6, 2 * TILE, KEEP), bf16),
            pltpu.VMEM((1024, 512), f32),
            pltpu.VMEM((1024, 512), f32),
            pltpu.VMEM((1024, SHARE), bf16),
            pltpu.VMEM((1024, KEEP), bf16),
            pltpu.VMEM((2, 1024, SHARE), bf16),
            pltpu.VMEM((2, 1024, KEEP), bf16),
            pltpu.VMEM((1024, SHARE), bf16),
            pltpu.VMEM((2, 1024, SHARE), bf16),
            pltpu.VMEM((2, 6, 2 * TILE, SHARE), bf16),
            pltpu.VMEM((2, 1024, SHARE), f32),
            pltpu.VMEM((2, 8, 512), f32),
            pltpu.VMEM((2, 8, 512), f32),
            dma((4,)),
            dma((2,)),
            dma((2,)),
            dma(()),
            dma(()),
            dma((3,)),
            dma((3,)),
            dma((6,)),
            dma((6,)),
            dma((6,)),
            dma((6,)),
            dma((2, 6)),
            dma((2, 6)),
            dma((2,)),
            dma((2,)),
            dma((2, 6)),
            dma((2, 6)),
            dma((2, 4)),
            dma((2, 4)),
            dma((2, 4)),
            dma((2, 4)),
            dma((2,)),
            dma((2,)),
        ],
        compiler_params=pltpu.CompilerParams(
            collective_id=0, has_side_effects=True, vmem_limit_bytes=56 << 20
        ),
        name="langevin_step",
    )(residual_flow, params, noise, down, heat, mate, mask)


def solution(mesh):
    placed = (
        P("dp", None),
        P("rep", None, "dp"),
        P("rep", None, "dp"),
        P("dp", None),
        P("rep"),
        P("rep"),
        P("rep"),
    )
    return jax.shard_map(
        body,
        mesh=mesh,
        in_specs=placed,
        out_specs=(P("rep", None, "dp"), P("rep", None, "dp")),
        check_vma=False,
    )
```

```python
import functools
import math

import jax
import jax.numpy as jnp
from jax import lax
from jax.experimental import pallas as pl
from jax.experimental.pallas import tpu as pltpu
from jax.sharding import PartitionSpec as P

MESH = pl.DeviceIdType.MESH
drift_stride = 0.5
TILE = 128
CHUNK = 256
SHARE = 256
KEEP = 512 - SHARE


def place():
    rep = lax.axis_index("rep")
    dp = lax.axis_index("dp")
    return rep, rep // 32, (rep // 16) % 2, rep % 16, dp // 2, dp % 2


def peers():
    rep, x, y_lo, z, y_hi, core = place()
    dp = y_hi * 2 + core

    def at(x, y_lo, y_hi, core):
        return ((x * 2 + y_lo) * 16 + z, y_hi * 2 + core)

    return {
        "sibling": at(x, y_lo, y_hi, 1 - core),
        "partner": at(x, y_lo, 1 - y_hi, core),
        "across": at(x, 1 - y_lo, 1 - y_hi, core),
        "x1": at((x + 1) % 4, y_lo, y_hi, core),
        "x2": at((x + 2) % 4, y_lo, y_hi, core),
        "x3": at((x + 3) % 4, y_lo, y_hi, core),
        "up": ((rep + 1) % 128, dp),
        "down": ((rep + 127) % 128, dp),
    }


def kernel(
    res_hbm,
    par_hbm,
    noise_hbm,
    down_hbm,
    heat,
    mate,
    mask,
    out_ref,
    gap_ref,
    res,
    par,
    noise,
    down,
    nrm,
    flip,
    flip_sib,
    slope,
    base,
    op_send,
    op_recv,
    hid,
    pg_send_b,
    pg_send_a,
    pg_b,
    pg_a,
    acc,
    rest,
    fresh_b,
    fresh_a,
    near_b,
    near_a,
    rest_send,
    rest_near,
    pg_near,
    acc_near,
    gap_sum,
    gap_recv,
    load_sem,
    swap_s,
    swap_r,
    quart_s,
    quart_r,
    spread_s,
    spread_r,
    flip_s,
    flip_r,
    op_s,
    op_r,
    pg_s,
    pg_r,
    w_s,
    w_r,
    zp_s,
    zp_r,
    za_s,
    za_r,
    zb_s,
    zb_r,
    gx_s,
    gx_r,
):
    factor = 1024 ** (-0.5)
    coeff = math.sqrt(2.0 / math.pi)
    rank, x = place()[:2]
    peer = peers()
    spot = rank % 4
    mixes = (spot != 0, spot != 3)
    sends = (spot != 3, spot != 0)
    ways = ("up", "down")
    turned = 2 - 2 * ((spot + 3) // 4)

    def remote(src, dst, send, recv, who):
        return pltpu.make_async_remote_copy(
            src_ref=src,
            dst_ref=dst,
            send_sem=send,
            recv_sem=recv,
            device_id=peer[who],
            device_id_type=MESH,
        )

    loads = [
        pltpu.make_async_copy(res_hbm, res.at[0], load_sem.at[0]),
        pltpu.make_async_copy(par_hbm.at[0], par.at[0], load_sem.at[1]),
        pltpu.make_async_copy(down_hbm, down.at[0], load_sem.at[2]),
        pltpu.make_async_copy(noise_hbm.at[0], noise, load_sem.at[3]),
    ]
    for copy in loads:
        copy.start()

    barrier = pltpu.get_barrier_semaphore()
    for who in peer:
        pl.semaphore_signal(barrier, inc=1, device_id=peer[who], device_id_type=MESH)
    pl.semaphore_wait(barrier, len(peer))

    quarter = pl.ds(pl.multiple_of(x * 96, 96), 96)
    loads[0].wait()
    quart = remote(res.at[0, quarter], res.at[1, quarter], quart_s, quart_r, "across")
    quart.start()
    loads[1].wait()
    swap_par = remote(par.at[0], par.at[1], swap_s.at[0], swap_r.at[0], "sibling")
    swap_par.start()
    loads[2].wait()
    swap_down = remote(down.at[0], down.at[1], swap_s.at[1], swap_r.at[1], "sibling")
    swap_down.start()

    def flip_copy(j):
        return remote(flip.at[j], flip_sib.at[j], flip_s.at[j], flip_r.at[j], "sibling")

    def op_copy(j):
        return remote(
            op_send.at[j], op_recv.at[(j + 3) % 6], op_s.at[j], op_r.at[(j + 3) % 6], "partner"
        )

    def pg_copies(j):
        low = pl.ds(TILE, TILE)
        return [
            remote(pg_send_b.at[j], pg_b.at[j, low], pg_s.at[0, j], pg_r.at[0, j], "sibling"),
            remote(pg_send_a.at[j], pg_a.at[j, low], pg_s.at[1, j], pg_r.at[1, j], "sibling"),
        ]

    def w_copy(side):
        return remote(rest_send, rest_near.at[side], w_s.at[side], w_r.at[side], ways[side])

    def zp_copy(side, j):
        return remote(
            pg_b.at[j], pg_near.at[side, j], zp_s.at[side, j], zp_r.at[side, j], ways[side]
        )

    def chunk(k):
        return pl.ds(pl.multiple_of(k * CHUNK, CHUNK), CHUNK)

    def za_copy(side, k):
        rows = chunk(k)
        return remote(
            fresh_a.at[rows], near_a.at[side, rows], za_s.at[side, k], za_r.at[side, k], ways[side]
        )

    def zb_copy(side, k):
        rows = chunk(k)
        return remote(
            fresh_b.at[rows], near_b.at[side, rows], zb_s.at[side, k], zb_r.at[side, k], ways[side]
        )

    def gx_copy(side):
        return remote(
            gap_sum.at[1 - side], gap_recv.at[side], gx_s.at[side], gx_r.at[side], ways[side]
        )

    def prepare(seq):
        def one(k, _):
            rows = pl.ds(pl.multiple_of(k * TILE, TILE), TILE)
            values = res[seq, rows, :].astype(jnp.float32)
            center = values - jnp.mean(values, axis=1, keepdims=True)
            spread = jnp.mean(center * center, axis=1, keepdims=True)
            nrm[seq * 3 + k] = (center * lax.rsqrt(spread + 1e-05)).astype(jnp.bfloat16)
            return 0

        lax.fori_loop(0, 3, one, 0)

    def step_ahead(seq):
        for c in range(4):
            cols = slice(c * CHUNK, (c + 1) * CHUNK)
            values = res[seq, :, cols].astype(jnp.float32)
            ahead = values - pltpu.roll(values, 383, 0)
            for k in range(3):
                base[seq * 3 + k, :, cols] = ahead[k * TILE : (k + 1) * TILE]

    def forward_in(j, side):
        rows = nrm[j]
        for c in range(2):
            cols = slice(c * CHUNK, (c + 1) * CHUNK)
            wide = slice(side * 512 + c * CHUNK, side * 512 + (c + 1) * CHUNK)
            v = jnp.dot(rows, par[side, :, cols], preferred_element_type=jnp.float32) * factor
            square = v * v
            tangent = jnp.tanh(coeff * v * (1.0 + 0.044715 * square))
            half = 0.5 * (1.0 + tangent)
            hid[:, wide] = (v * half).astype(jnp.bfloat16)
            slope[j, :, wide] = half + 0.5 * coeff * v * (1.0 - tangent * tangent) * (
                1.0 + 3.0 * 0.044715 * square
            )

    def forward_out(j):
        for c in range(4):
            wide = slice(c * CHUNK, (c + 1) * CHUNK)
            part = jnp.dot(
                hid[:, :512], down[0, :, wide], preferred_element_type=jnp.float32
            ) + jnp.dot(hid[:, 512:], down[1, :, wide], preferred_element_type=jnp.float32)
            base[j, :, wide] += part
            op_send[j, :, wide] = part.astype(jnp.bfloat16)
        op_copy(j).start()

    def forward(j, _):
        forward_in(j, 0)
        forward_in(j, 1)
        forward_out(j)
        return 0

    def turn(j, _):
        flip[j] = nrm[j].T
        flip_copy(j).start()
        return 0

    loads[3].wait()
    heat_root = jnp.sqrt(jnp.full((1, 512), 2.0 * drift_stride * heat[0], jnp.float32))

    def keep(k, _):
        rows = pl.ds(pl.multiple_of(k * TILE, TILE), TILE)
        current = par[0, rows, :].astype(jnp.float32)
        still = current - drift_stride * current + heat_root * noise[rows, :].astype(jnp.float32)
        rest[rows, :] = still
        rest_send[rows, :] = still[:, :SHARE].astype(jnp.bfloat16)
        return 0

    prepare(0)
    step_ahead(0)
    forward_in(0, 0)
    lax.fori_loop(0, 8, keep, 0)
    for side in range(2):
        pl.when(sends[side])(w_copy(side).start)
    swap_par.wait_recv()
    forward_in(0, 1)
    swap_down.wait_recv()
    forward_out(0)
    quart.wait_recv()
    spreads = [
        remote(
            res.at[1, quarter], res.at[1, quarter], spread_s.at[k - 1], spread_r.at[k - 1], f"x{k}"
        )
        for k in (1, 2, 3)
    ]
    for copy in spreads:
        copy.start()
    lax.fori_loop(1, 3, forward, 0)
    lax.fori_loop(0, 3, turn, 0)

    for copy in spreads:
        copy.wait_recv()
    prepare(1)
    step_ahead(1)
    lax.fori_loop(3, 6, forward, 0)
    lax.fori_loop(3, 6, turn, 0)

    def backward(j):
        op_copy((j + 3) % 6).wait_recv()
        keepers = lax.broadcasted_iota(jnp.int32, (TILE, 1), 0) + (j % 3) * TILE < 383
        errors = jnp.where(keepers, base[j] + op_recv[j].astype(jnp.float32), 0.0).astype(
            jnp.bfloat16
        )
        for side in (1, 0):
            grad = lax.dot_general(
                errors, down[side], (((1,), (1,)), ((), ())), preferred_element_type=jnp.float32
            )
            grad = (grad * slope[j, :, side * 512 : side * 512 + 512]).astype(jnp.bfloat16)
            if side == 1:
                pg_send_b[j] = grad[:, :SHARE]
                pg_send_a[j] = grad[:, SHARE:]
                for copy in pg_copies(j):
                    copy.start()
            else:
                pg_b[j, :TILE] = grad[:, :SHARE]
                pg_a[j, :TILE] = grad[:, SHARE:]

    def arrive(j):
        for copy in pg_copies(j):
            copy.wait_recv()
        for side in range(2):
            pl.when(sends[side])(zp_copy(side, j).start)
        flip_copy(j).wait_recv()

    def joined(tiles, rows):
        pieces = []
        for j in tiles:
            pieces += [flip[j, rows, :], flip_sib[j, rows, :]]
        return jnp.concatenate(pieces, axis=1)

    def product(tiles, k):
        right = jnp.concatenate(
            [
                pg_b[tiles[0] : tiles[-1] + 1].reshape(2 * TILE * len(tiles), SHARE),
                pg_a[tiles[0] : tiles[-1] + 1].reshape(2 * TILE * len(tiles), KEEP),
            ],
            axis=1,
        )
        return jnp.dot(joined(tiles, chunk(k)), right, preferred_element_type=jnp.float32)

    def gather_near(tiles, fresh_start):
        for side in range(2):

            @pl.when(mixes[side])
            def _():
                for j in tiles:
                    zp_copy(side, j).wait_recv()

                def one(k, _):
                    right = pg_near[side, tiles[0] : tiles[-1] + 1].reshape(
                        2 * TILE * len(tiles), SHARE
                    )
                    more = jnp.dot(
                        joined(tiles, chunk(k)), right, preferred_element_type=jnp.float32
                    )
                    if fresh_start:
                        acc_near[side, chunk(k), :] = more
                    else:
                        near_b[side, chunk(k), :] = (
                            rest_near[side, chunk(k), :].astype(jnp.float32)
                            - (drift_stride * factor) * (acc_near[side, chunk(k), :] + more)
                        ).astype(jnp.bfloat16)
                    return 0

                if not fresh_start:
                    w_copy(side).wait_recv()
                lax.fori_loop(0, 4, one, 0)

    def first_sum(k, _):
        acc[chunk(k), :] = product((3, 4, 5), k)
        return 0

    def second_sum(k, _):
        acc[chunk(k), :] += product((0, 1), k)
        return 0

    backward(3)
    backward(4)
    arrive(3)
    backward(5)
    arrive(4)
    backward(0)
    arrive(5)
    lax.fori_loop(0, 4, first_sum, 0)
    backward(1)
    arrive(0)
    gather_near((3, 4, 5), True)
    backward(2)
    arrive(1)
    lax.fori_loop(0, 4, second_sum, 0)
    arrive(2)

    for k in range(4):
        rows = chunk((k + turned) % 4)
        total = acc[rows, :] + product((2,), (k + turned) % 4)
        moved = (rest[rows, :] - (drift_stride * factor) * total).astype(jnp.bfloat16)
        fresh_b[rows, :] = moved[:, :SHARE]
        fresh_a[rows, :] = moved[:, SHARE:]
        for side in range(2):
            pl.when(sends[side])(za_copy(side, (k + turned) % 4).start)
            if k < 2:

                @pl.when(jnp.logical_not(sends[side]))
                def _():
                    za_copy(side, (k + turned) % 4).start()
                    zb_copy(side, (k + turned) % 4).start()

    gather_near((0, 1, 2), False)

    taken = jnp.full((1, 512), mask[0], jnp.int32) == 1
    mates = jnp.full((1, 512), mate[0], jnp.int32)
    picks = (taken & (mates == rank - 1), taken & (mates == rank + 1))
    gap_sum[...] = jnp.zeros((2, 8, 512), jnp.float32)
    pairs = ((0, SHARE, fresh_b, near_b), (SHARE, 512, fresh_a, near_a))

    def add_gap(side, k):
        for first, last, own_ref, near_ref in pairs:
            gap = own_ref[chunk(k), :].astype(jnp.float32) - near_ref[side, chunk(k), :].astype(
                jnp.float32
            )
            gap_sum[side, :, first:last] += jnp.sum(
                (gap * gap).reshape(CHUNK // 8, 8, last - first), axis=0
            )

    for side in range(2):

        @pl.when(jnp.logical_not(mixes[side]))
        def _():
            for k in (2 * side, 2 * side + 1):
                za_copy(side, k).wait_recv()
                zb_copy(side, k).wait_recv()
                add_gap(side, k)
            gx_copy(1 - side).start()

    def mix(k, _):
        for side in range(2):

            @pl.when(mixes[side])
            def _():
                za_copy(side, k).wait_recv()
                add_gap(side, k)

        for first, last, own_ref, near_ref in pairs:
            out_ref[0, chunk(k), first:last] = jnp.where(
                picks[0][:, first:last],
                near_ref[0, chunk(k), :],
                jnp.where(
                    picks[1][:, first:last], near_ref[1, chunk(k), :], own_ref[chunk(k), :]
                ),
            )
        return 0

    lax.fori_loop(0, 4, mix, 0)

    for side in range(2):

        @pl.when(jnp.logical_not(mixes[side]))
        def _():
            gx_copy(side).wait_recv()
            gap_recv[side] += gap_sum[side]
            gap_ref[0, side : side + 1, :] = jnp.sum(gap_recv[side], axis=0, keepdims=True) * (
                1.0 / 1024.0
            )

        @pl.when(mixes[side])
        def _():
            gap_ref[0, side : side + 1, :] = jnp.sum(gap_sum[side], axis=0, keepdims=True) * (
                1.0 / 1024.0
            )

    quart.wait_send()
    swap_par.wait_send()
    swap_down.wait_send()
    for copy in spreads:
        copy.wait_send()

    def finish(j, _):
        flip_copy(j).wait_send()
        op_copy(j).wait_send()
        for copy in pg_copies(j):
            copy.wait_send()
        for side in range(2):
            pl.when(sends[side])(zp_copy(side, j).wait_send)
        return 0

    lax.fori_loop(0, 6, finish, 0)
    for side in range(2):

        @pl.when(sends[side])
        def _():
            w_copy(side).wait_send()
            for k in range(4):
                za_copy(side, k).wait_send()

        @pl.when(jnp.logical_not(sends[side]))
        def _():
            gx_copy(side).wait_send()
            for k in (2 * side, 2 * side + 1):
                za_copy(side, k).wait_send()
                zb_copy(side, k).wait_send()


def body(residual_flow, params, noise, down, heat, mate, mask):
    any_spec = pl.BlockSpec(memory_space=pl.ANY)
    scalar = pl.BlockSpec(memory_space=pltpu.SMEM)
    vmem = pl.BlockSpec(memory_space=pltpu.VMEM)
    bf16, f32 = jnp.bfloat16, jnp.float32
    dma = pltpu.SemaphoreType.DMA
    return pl.pallas_call(
        kernel,
        out_shape=(
            jax.ShapeDtypeStruct((1, 1024, 512), bf16),
            jax.ShapeDtypeStruct((1, 2, 512), f32),
        ),
        in_specs=[any_spec] * 4 + [scalar] * 3,
        out_specs=(vmem, vmem),
        scratch_shapes=[
            pltpu.VMEM((2, 384, 1024), bf16),
            pltpu.VMEM((2, 1024, 512), bf16),
            pltpu.VMEM((1024, 512), bf16),
            pltpu.VMEM((2, 512, 1024), bf16),
            pltpu.VMEM((6, TILE, 1024), bf16),
            pltpu.VMEM((6, 1024, TILE), bf16),
            pltpu.VMEM((6, 1024, TILE), bf16),
            pltpu.VMEM((6, TILE, 1024), f32),
            pltpu.VMEM((6, TILE, 1024), f32),
            pltpu.VMEM((6, TILE, 1024), bf16),
            pltpu.VMEM((6, TILE, 1024), bf16),
            pltpu.VMEM((TILE, 1024), bf16),
            pltpu.VMEM((6, TILE, SHARE), bf16),
            pltpu.VMEM((6, TILE, KEEP), bf16),
            pltpu.VMEM((6, 2 * TILE, SHARE), bf16),
            pltpu.VMEM((6, 2 * TILE, KEEP), bf16),
            pltpu.VMEM((1024, 512), f32),
            pltpu.VMEM((1024, 512), f32),
            pltpu.VMEM((1024, SHARE), bf16),
            pltpu.VMEM((1024, KEEP), bf16),
            pltpu.VMEM((2, 1024, SHARE), bf16),
            pltpu.VMEM((2, 1024, KEEP), bf16),
            pltpu.VMEM((1024, SHARE), bf16),
            pltpu.VMEM((2, 1024, SHARE), bf16),
            pltpu.VMEM((2, 6, 2 * TILE, SHARE), bf16),
            pltpu.VMEM((2, 1024, SHARE), f32),
            pltpu.VMEM((2, 8, 512), f32),
            pltpu.VMEM((2, 8, 512), f32),
            dma((4,)),
            dma((2,)),
            dma((2,)),
            dma(()),
            dma(()),
            dma((3,)),
            dma((3,)),
            dma((6,)),
            dma((6,)),
            dma((6,)),
            dma((6,)),
            dma((2, 6)),
            dma((2, 6)),
            dma((2,)),
            dma((2,)),
            dma((2, 6)),
            dma((2, 6)),
            dma((2, 4)),
            dma((2, 4)),
            dma((2, 4)),
            dma((2, 4)),
            dma((2,)),
            dma((2,)),
        ],
        compiler_params=pltpu.CompilerParams(
            collective_id=0, has_side_effects=True, vmem_limit_bytes=52 << 20
        ),
        name="langevin_step",
    )(
        *(
            pltpu.with_memory_space_constraint(each, pltpu.HBM)
            for each in (residual_flow, params, noise, down)
        ),
        heat,
        mate,
        mask,
    )


def solution(mesh):
    placed = (
        P("dp", None),
        P("rep", None, "dp"),
        P("rep", None, "dp"),
        P("dp", None),
        P("rep"),
        P("rep"),
        P("rep"),
    )
    return jax.shard_map(
        body,
        mesh=mesh,
        in_specs=placed,
        out_specs=(P("rep", None, "dp"), P("rep", None, "dp")),
        check_vma=False,
    )
```

```python
import functools
import math

import jax
import jax.numpy as jnp
from jax import lax
from jax.experimental import pallas as pl
from jax.experimental.pallas import tpu as pltpu
from jax.sharding import PartitionSpec as P

MESH = pl.DeviceIdType.MESH
drift_stride = 0.5
TILE = 128
CHUNK = 256
SHARE = 256
KEEP = 512 - SHARE
EDGE = (((0, 256), (256, 448), (448, 576)), ((768, 1024), (576, 768), (448, 576)))


def place():
    rep = lax.axis_index("rep")
    dp = lax.axis_index("dp")
    return rep, rep // 32, (rep // 16) % 2, rep % 16, dp // 2, dp % 2


def peers():
    rep, x, y_lo, z, y_hi, core = place()
    dp = y_hi * 2 + core

    def at(x, y_lo, y_hi, core):
        return ((x * 2 + y_lo) * 16 + z, y_hi * 2 + core)

    return {
        "sibling": at(x, y_lo, y_hi, 1 - core),
        "partner": at(x, y_lo, 1 - y_hi, core),
        "across": at(x, 1 - y_lo, 1 - y_hi, core),
        "x1": at((x + 1) % 4, y_lo, y_hi, core),
        "x2": at((x + 2) % 4, y_lo, y_hi, core),
        "x3": at((x + 3) % 4, y_lo, y_hi, core),
        "up": ((rep + 1) % 128, dp),
        "down": ((rep + 127) % 128, dp),
    }


def kernel(
    res_hbm,
    par_hbm,
    noise_hbm,
    down_hbm,
    heat,
    mate,
    mask,
    out_ref,
    gap_ref,
    res,
    par,
    noise,
    down,
    nrm,
    flip,
    flip_sib,
    slope,
    base,
    op_send,
    op_recv,
    hid,
    pg_send_b,
    pg_send_a,
    pg_b,
    pg_a,
    acc,
    rest,
    fresh_b,
    fresh_a,
    near_b,
    near_a,
    rest_send,
    rest_near,
    pg_near,
    acc_near,
    gap_sum,
    gap_send,
    gap_recv,
    load_sem,
    swap_s,
    swap_r,
    quart_s,
    quart_r,
    spread_s,
    spread_r,
    flip_s,
    flip_r,
    op_s,
    op_r,
    pg_s,
    pg_r,
    w_s,
    w_r,
    zp_s,
    zp_r,
    za_s,
    za_r,
    zb_s,
    zb_r,
    gx_s,
    gx_r,
):
    factor = 1024 ** (-0.5)
    coeff = math.sqrt(2.0 / math.pi)
    rank, x = place()[:2]
    peer = peers()
    spot = rank % 4
    mixes = (spot != 0, spot != 3)
    sends = (spot != 3, spot != 0)
    ways = ("up", "down")
    turned = 2 - 2 * ((spot + 3) // 4)

    def remote(src, dst, send, recv, who):
        return pltpu.make_async_remote_copy(
            src_ref=src,
            dst_ref=dst,
            send_sem=send,
            recv_sem=recv,
            device_id=peer[who],
            device_id_type=MESH,
        )

    loads = [
        pltpu.make_async_copy(res_hbm, res.at[0], load_sem.at[0]),
        pltpu.make_async_copy(par_hbm.at[0], par.at[0], load_sem.at[1]),
        pltpu.make_async_copy(down_hbm, down.at[0], load_sem.at[2]),
        pltpu.make_async_copy(noise_hbm.at[0], noise, load_sem.at[3]),
    ]
    for copy in loads:
        copy.start()

    barrier = pltpu.get_barrier_semaphore()
    for who in peer:
        pl.semaphore_signal(barrier, inc=1, device_id=peer[who], device_id_type=MESH)
    pl.semaphore_wait(barrier, len(peer))

    quarter = pl.ds(pl.multiple_of(x * 96, 96), 96)
    loads[0].wait()
    quart = remote(res.at[0, quarter], res.at[1, quarter], quart_s, quart_r, "across")
    quart.start()
    loads[1].wait()
    swap_par = remote(par.at[0], par.at[1], swap_s.at[0], swap_r.at[0], "sibling")
    swap_par.start()
    loads[2].wait()
    swap_down = remote(down.at[0], down.at[1], swap_s.at[1], swap_r.at[1], "sibling")
    swap_down.start()

    def flip_copy(j):
        return remote(flip.at[j], flip_sib.at[j], flip_s.at[j], flip_r.at[j], "sibling")

    def op_copy(j):
        return remote(
            op_send.at[j], op_recv.at[(j + 3) % 6], op_s.at[j], op_r.at[(j + 3) % 6], "partner"
        )

    def pg_copies(j):
        low = pl.ds(TILE, TILE)
        return [
            remote(pg_send_b.at[j], pg_b.at[j, low], pg_s.at[0, j], pg_r.at[0, j], "sibling"),
            remote(pg_send_a.at[j], pg_a.at[j, low], pg_s.at[1, j], pg_r.at[1, j], "sibling"),
        ]

    def w_copy(side):
        return remote(rest_send, rest_near.at[side], w_s.at[side], w_r.at[side], ways[side])

    def zp_copy(side, j):
        return remote(
            pg_b.at[j], pg_near.at[side, j], zp_s.at[side, j], zp_r.at[side, j], ways[side]
        )

    def chunk(k):
        return pl.ds(pl.multiple_of(k * CHUNK, CHUNK), CHUNK)

    def za_copy(side, k):
        rows = chunk(k)
        return remote(
            fresh_a.at[rows], near_a.at[side, rows], za_s.at[side, k], za_r.at[side, k], ways[side]
        )

    def edge_copies(side, k):
        rows = slice(*EDGE[side][k])
        return [
            remote(
                fresh_a.at[rows],
                near_a.at[side, rows],
                za_s.at[side, k],
                za_r.at[side, k],
                ways[side],
            ),
            remote(
                fresh_b.at[rows],
                near_b.at[side, rows],
                zb_s.at[side, k],
                zb_r.at[side, k],
                ways[side],
            ),
        ]

    def gx_copy(side):
        return remote(
            gap_send.at[1 - side], gap_recv.at[side], gx_s.at[side], gx_r.at[side], ways[side]
        )

    def prepare(seq):
        def one(k, _):
            rows = pl.ds(pl.multiple_of(k * TILE, TILE), TILE)
            values = res[seq, rows, :].astype(jnp.float32)
            center = values - jnp.mean(values, axis=1, keepdims=True)
            spread = jnp.mean(center * center, axis=1, keepdims=True)
            nrm[seq * 3 + k] = (center * lax.rsqrt(spread + 1e-05)).astype(jnp.bfloat16)
            return 0

        lax.fori_loop(0, 3, one, 0)

    def step_ahead(seq):
        for c in range(4):
            cols = slice(c * CHUNK, (c + 1) * CHUNK)
            values = res[seq, :, cols].astype(jnp.float32)
            ahead = values - pltpu.roll(values, 383, 0)
            for k in range(3):
                base[seq * 3 + k, :, cols] = ahead[k * TILE : (k + 1) * TILE]

    def forward_in(j, side):
        rows = nrm[j]
        for c in range(2):
            cols = slice(c * CHUNK, (c + 1) * CHUNK)
            wide = slice(side * 512 + c * CHUNK, side * 512 + (c + 1) * CHUNK)
            v = jnp.dot(rows, par[side, :, cols], preferred_element_type=jnp.float32) * factor
            square = v * v
            tangent = jnp.tanh(coeff * v * (1.0 + 0.044715 * square))
            half = 0.5 * (1.0 + tangent)
            hid[:, wide] = (v * half).astype(jnp.bfloat16)
            slope[j, :, wide] = half + 0.5 * coeff * v * (1.0 - tangent * tangent) * (
                1.0 + 3.0 * 0.044715 * square
            )

    def forward_out(j):
        for c in range(4):
            wide = slice(c * CHUNK, (c + 1) * CHUNK)
            part = jnp.dot(
                hid[:, :512], down[0, :, wide], preferred_element_type=jnp.float32
            ) + jnp.dot(hid[:, 512:], down[1, :, wide], preferred_element_type=jnp.float32)
            base[j, :, wide] += part
            op_send[j, :, wide] = part.astype(jnp.bfloat16)
        op_copy(j).start()

    def forward(j, _):
        forward_in(j, 0)
        forward_in(j, 1)
        forward_out(j)
        return 0

    def turn(j, _):
        flip[j] = nrm[j].T
        flip_copy(j).start()
        return 0

    loads[3].wait()
    heat_root = jnp.sqrt(jnp.full((1, 512), 2.0 * drift_stride * heat[0], jnp.float32))

    def keep(k, _):
        rows = pl.ds(pl.multiple_of(k * TILE, TILE), TILE)
        current = par[0, rows, :].astype(jnp.float32)
        still = current - drift_stride * current + heat_root * noise[rows, :].astype(jnp.float32)
        rest[rows, :] = still
        rest_send[rows, :] = still[:, :SHARE].astype(jnp.bfloat16)
        return 0

    prepare(0)
    step_ahead(0)
    forward_in(0, 0)
    lax.fori_loop(0, 8, keep, 0)
    for side in range(2):
        pl.when(sends[side])(w_copy(side).start)
    swap_par.wait_recv()
    forward_in(0, 1)
    swap_down.wait_recv()
    forward_out(0)
    quart.wait_recv()
    spreads = [
        remote(
            res.at[1, quarter], res.at[1, quarter], spread_s.at[k - 1], spread_r.at[k - 1], f"x{k}"
        )
        for k in (1, 2, 3)
    ]
    for copy in spreads:
        copy.start()
    lax.fori_loop(1, 3, forward, 0)
    lax.fori_loop(0, 3, turn, 0)

    for copy in spreads:
        copy.wait_recv()
    prepare(1)
    step_ahead(1)
    lax.fori_loop(3, 6, forward, 0)
    lax.fori_loop(3, 6, turn, 0)

    def backward(j):
        op_copy((j + 3) % 6).wait_recv()
        keepers = lax.broadcasted_iota(jnp.int32, (TILE, 1), 0) + (j % 3) * TILE < 383
        errors = jnp.where(keepers, base[j] + op_recv[j].astype(jnp.float32), 0.0).astype(
            jnp.bfloat16
        )
        for side in (1, 0):
            grad = lax.dot_general(
                errors, down[side], (((1,), (1,)), ((), ())), preferred_element_type=jnp.float32
            )
            grad = (grad * slope[j, :, side * 512 : side * 512 + 512]).astype(jnp.bfloat16)
            if side == 1:
                pg_send_b[j] = grad[:, :SHARE]
                pg_send_a[j] = grad[:, SHARE:]
                for copy in pg_copies(j):
                    copy.start()
            else:
                pg_b[j, :TILE] = grad[:, :SHARE]
                pg_a[j, :TILE] = grad[:, SHARE:]

    def arrive(j):
        for copy in pg_copies(j):
            copy.wait_recv()
        for side in range(2):
            pl.when(sends[side])(zp_copy(side, j).start)
        flip_copy(j).wait_recv()

    def joined(tiles, rows):
        pieces = []
        for j in tiles:
            pieces += [flip[j, rows, :], flip_sib[j, rows, :]]
        return jnp.concatenate(pieces, axis=1)

    def product(tiles, k):
        right = jnp.concatenate(
            [
                pg_b[tiles[0] : tiles[-1] + 1].reshape(2 * TILE * len(tiles), SHARE),
                pg_a[tiles[0] : tiles[-1] + 1].reshape(2 * TILE * len(tiles), KEEP),
            ],
            axis=1,
        )
        return jnp.dot(joined(tiles, chunk(k)), right, preferred_element_type=jnp.float32)

    def gather_near(tiles, fresh_start):
        for side in range(2):

            @pl.when(mixes[side])
            def _():
                for j in tiles:
                    zp_copy(side, j).wait_recv()

                def one(k, _):
                    right = pg_near[side, tiles[0] : tiles[-1] + 1].reshape(
                        2 * TILE * len(tiles), SHARE
                    )
                    more = jnp.dot(
                        joined(tiles, chunk(k)), right, preferred_element_type=jnp.float32
                    )
                    if fresh_start:
                        acc_near[side, chunk(k), :] = more
                    else:
                        near_b[side, chunk(k), :] = (
                            rest_near[side, chunk(k), :].astype(jnp.float32)
                            - (drift_stride * factor) * (acc_near[side, chunk(k), :] + more)
                        ).astype(jnp.bfloat16)
                    return 0

                if not fresh_start:
                    w_copy(side).wait_recv()
                lax.fori_loop(0, 4, one, 0)

    def first_sum(k, _):
        acc[chunk(k), :] = product((3, 4, 5), k)
        return 0

    def second_sum(k, _):
        acc[chunk(k), :] += product((0, 1), k)
        return 0

    backward(3)
    backward(4)
    arrive(3)
    backward(5)
    arrive(4)
    arrive(5)
    lax.fori_loop(0, 4, first_sum, 0)
    backward(0)
    arrive(0)
    gather_near((3, 4, 5), True)
    backward(1)
    arrive(1)
    lax.fori_loop(0, 4, second_sum, 0)
    backward(2)
    arrive(2)

    for k in range(4):
        rows = chunk((k + turned) % 4)
        total = acc[rows, :] + product((2,), (k + turned) % 4)
        moved = (rest[rows, :] - (drift_stride * factor) * total).astype(jnp.bfloat16)
        fresh_b[rows, :] = moved[:, :SHARE]
        fresh_a[rows, :] = moved[:, SHARE:]
        for side in range(2):
            pl.when(sends[side])(za_copy(side, (k + turned) % 4).start)
            if k in (1, 3):

                @pl.when(jnp.logical_not(sends[side]))
                def _():
                    for piece in ((0, 1), (2,))[k // 2]:
                        for copy in edge_copies(side, piece):
                            copy.start()

    gather_near((0, 1, 2), False)

    taken = jnp.full((1, 512), mask[0], jnp.int32) == 1
    mates = jnp.full((1, 512), mate[0], jnp.int32)
    picks = (taken & (mates == rank - 1), taken & (mates == rank + 1))
    gap_sum[...] = jnp.zeros((2, 8, 512), jnp.float32)
    pairs = ((0, SHARE, fresh_b, near_b), (SHARE, 512, fresh_a, near_a))

    def add_gap(side, rows, count):
        for first, last, own_ref, near_ref in pairs:
            gap = own_ref[rows, :].astype(jnp.float32) - near_ref[side, rows, :].astype(
                jnp.float32
            )
            gap_sum[side, :, first:last] += jnp.sum(
                (gap * gap).reshape(count // 8, 8, last - first), axis=0
            )

    for side in range(2):

        @pl.when(jnp.logical_not(mixes[side]))
        def _():
            for piece in (0, 1):
                for copy in edge_copies(side, piece):
                    copy.wait_recv()
                first, last = EDGE[side][piece]
                add_gap(side, slice(first, last), last - first)
            gap_send[side] = gap_sum[side]
            gx_copy(1 - side).start()

    def mix(k, _):
        for side in range(2):

            @pl.when(mixes[side])
            def _():
                za_copy(side, k).wait_recv()
                add_gap(side, chunk(k), CHUNK)

        def choose(sides):
            for first, last, own_ref, near_ref in pairs:
                value = own_ref[chunk(k), :]
                for side in sides:
                    value = jnp.where(
                        picks[side][:, first:last], near_ref[side, chunk(k), :], value
                    )
                out_ref[0, chunk(k), first:last] = value

        pl.when(mixes[0] & mixes[1])(lambda: choose((0, 1)))
        pl.when(jnp.logical_not(mixes[0]))(lambda: choose((1,)))
        pl.when(jnp.logical_not(mixes[1]))(lambda: choose((0,)))
        return 0

    lax.fori_loop(0, 4, mix, 0)

    for side in range(2):

        @pl.when(jnp.logical_not(mixes[side]))
        def _():
            for copy in edge_copies(side, 2):
                copy.wait_recv()
            first, last = EDGE[side][2]
            add_gap(side, slice(first, last), last - first)
            gx_copy(side).wait_recv()
            gap_recv[side] += gap_sum[side]
            gap_ref[0, side : side + 1, :] = jnp.sum(gap_recv[side], axis=0, keepdims=True) * (
                1.0 / 1024.0
            )

        @pl.when(mixes[side])
        def _():
            gap_ref[0, side : side + 1, :] = jnp.sum(gap_sum[side], axis=0, keepdims=True) * (
                1.0 / 1024.0
            )

    quart.wait_send()
    swap_par.wait_send()
    swap_down.wait_send()
    for copy in spreads:
        copy.wait_send()

    def finish(j, _):
        flip_copy(j).wait_send()
        op_copy(j).wait_send()
        for copy in pg_copies(j):
            copy.wait_send()
        for side in range(2):
            pl.when(sends[side])(zp_copy(side, j).wait_send)
        return 0

    lax.fori_loop(0, 6, finish, 0)
    for side in range(2):

        @pl.when(sends[side])
        def _():
            w_copy(side).wait_send()
            for k in range(4):
                za_copy(side, k).wait_send()

        @pl.when(jnp.logical_not(sends[side]))
        def _():
            gx_copy(side).wait_send()
            for piece in range(3):
                for copy in edge_copies(side, piece):
                    copy.wait_send()


def body(residual_flow, params, noise, down, heat, mate, mask):
    any_spec = pl.BlockSpec(memory_space=pl.ANY)
    scalar = pl.BlockSpec(memory_space=pltpu.SMEM)
    vmem = pl.BlockSpec(memory_space=pltpu.VMEM)
    bf16, f32 = jnp.bfloat16, jnp.float32
    dma = pltpu.SemaphoreType.DMA
    return pl.pallas_call(
        kernel,
        out_shape=(
            jax.ShapeDtypeStruct((1, 1024, 512), bf16),
            jax.ShapeDtypeStruct((1, 2, 512), f32),
        ),
        in_specs=[any_spec] * 4 + [scalar] * 3,
        out_specs=(vmem, vmem),
        scratch_shapes=[
            pltpu.VMEM((2, 384, 1024), bf16),
            pltpu.VMEM((2, 1024, 512), bf16),
            pltpu.VMEM((1024, 512), bf16),
            pltpu.VMEM((2, 512, 1024), bf16),
            pltpu.VMEM((6, TILE, 1024), bf16),
            pltpu.VMEM((6, 1024, TILE), bf16),
            pltpu.VMEM((6, 1024, TILE), bf16),
            pltpu.VMEM((6, TILE, 1024), f32),
            pltpu.VMEM((6, TILE, 1024), f32),
            pltpu.VMEM((6, TILE, 1024), bf16),
            pltpu.VMEM((6, TILE, 1024), bf16),
            pltpu.VMEM((TILE, 1024), bf16),
            pltpu.VMEM((6, TILE, SHARE), bf16),
            pltpu.VMEM((6, TILE, KEEP), bf16),
            pltpu.VMEM((6, 2 * TILE, SHARE), bf16),
            pltpu.VMEM((6, 2 * TILE, KEEP), bf16),
            pltpu.VMEM((1024, 512), f32),
            pltpu.VMEM((1024, 512), f32),
            pltpu.VMEM((1024, SHARE), bf16),
            pltpu.VMEM((1024, KEEP), bf16),
            pltpu.VMEM((2, 1024, SHARE), bf16),
            pltpu.VMEM((2, 1024, KEEP), bf16),
            pltpu.VMEM((1024, SHARE), bf16),
            pltpu.VMEM((2, 1024, SHARE), bf16),
            pltpu.VMEM((2, 6, 2 * TILE, SHARE), bf16),
            pltpu.VMEM((2, 1024, SHARE), f32),
            pltpu.VMEM((2, 8, 512), f32),
            pltpu.VMEM((2, 8, 512), f32),
            pltpu.VMEM((2, 8, 512), f32),
            dma((4,)),
            dma((2,)),
            dma((2,)),
            dma(()),
            dma(()),
            dma((3,)),
            dma((3,)),
            dma((6,)),
            dma((6,)),
            dma((6,)),
            dma((6,)),
            dma((2, 6)),
            dma((2, 6)),
            dma((2,)),
            dma((2,)),
            dma((2, 6)),
            dma((2, 6)),
            dma((2, 4)),
            dma((2, 4)),
            dma((2, 4)),
            dma((2, 4)),
            dma((2,)),
            dma((2,)),
        ],
        compiler_params=pltpu.CompilerParams(
            collective_id=0, has_side_effects=True, vmem_limit_bytes=52 << 20
        ),
        name="langevin_step",
    )(
        *(
            pltpu.with_memory_space_constraint(each, pltpu.HBM)
            for each in (residual_flow, params, noise, down)
        ),
        heat,
        mate,
        mask,
    )


def solution(mesh):
    placed = (
        P("dp", None),
        P("rep", None, "dp"),
        P("rep", None, "dp"),
        P("dp", None),
        P("rep"),
        P("rep"),
        P("rep"),
    )
    return jax.shard_map(
        body,
        mesh=mesh,
        in_specs=placed,
        out_specs=(P("rep", None, "dp"), P("rep", None, "dp")),
        check_vma=False,
    )
```

```python
import functools
import math

import jax
import jax.numpy as jnp
from jax import lax
from jax.experimental import pallas as pl
from jax.experimental.pallas import tpu as pltpu
from jax.sharding import PartitionSpec as P

MESH = pl.DeviceIdType.MESH
drift_stride = 0.5
TILE = 128
CHUNK = 256
SHARE = 256
KEEP = 512 - SHARE
EDGE = (((0, 256), (256, 416), (416, 608)), ((768, 1024), (608, 768), (416, 608)))


def place():
    rep = lax.axis_index("rep")
    dp = lax.axis_index("dp")
    return rep, rep // 32, (rep // 16) % 2, rep % 16, dp // 2, dp % 2


def peers():
    rep, x, y_lo, z, y_hi, core = place()
    dp = y_hi * 2 + core

    def at(x, y_lo, y_hi, core):
        return ((x * 2 + y_lo) * 16 + z, y_hi * 2 + core)

    return {
        "sibling": at(x, y_lo, y_hi, 1 - core),
        "partner": at(x, y_lo, 1 - y_hi, core),
        "across": at(x, 1 - y_lo, 1 - y_hi, core),
        "x1": at((x + 1) % 4, y_lo, y_hi, core),
        "x2": at((x + 2) % 4, y_lo, y_hi, core),
        "x3": at((x + 3) % 4, y_lo, y_hi, core),
        "up": ((rep + 1) % 128, dp),
        "down": ((rep + 127) % 128, dp),
    }


def kernel(
    res_hbm,
    par_hbm,
    noise_hbm,
    down_hbm,
    heat,
    mate,
    mask,
    out_ref,
    gap_ref,
    res,
    par,
    noise,
    down,
    nrm,
    flip,
    flip_sib,
    slope,
    base,
    op_send,
    op_recv,
    hid,
    pg_send_b,
    pg_send_a,
    pg_b,
    pg_a,
    acc,
    rest,
    fresh_b,
    fresh_a,
    near_b,
    near_a,
    rest_send,
    rest_near,
    pg_near,
    acc_near,
    gap_sum,
    gap_send,
    gap_recv,
    load_sem,
    swap_s,
    swap_r,
    quart_s,
    quart_r,
    spread_s,
    spread_r,
    flip_s,
    flip_r,
    op_s,
    op_r,
    pg_s,
    pg_r,
    w_s,
    w_r,
    zp_s,
    zp_r,
    za_s,
    za_r,
    zb_s,
    zb_r,
    gx_s,
    gx_r,
):
    factor = 1024 ** (-0.5)
    coeff = math.sqrt(2.0 / math.pi)
    rank, x = place()[:2]
    peer = peers()
    spot = rank % 4
    mixes = (spot != 0, spot != 3)
    sends = (spot != 3, spot != 0)
    ways = ("up", "down")
    turned = 2 - 2 * ((spot + 3) // 4)

    def remote(src, dst, send, recv, who):
        return pltpu.make_async_remote_copy(
            src_ref=src,
            dst_ref=dst,
            send_sem=send,
            recv_sem=recv,
            device_id=peer[who],
            device_id_type=MESH,
        )

    loads = [
        pltpu.make_async_copy(res_hbm, res.at[0], load_sem.at[0]),
        pltpu.make_async_copy(par_hbm.at[0], par.at[0], load_sem.at[1]),
        pltpu.make_async_copy(down_hbm, down.at[0], load_sem.at[2]),
        pltpu.make_async_copy(noise_hbm.at[0], noise, load_sem.at[3]),
    ]
    for copy in loads:
        copy.start()

    barrier = pltpu.get_barrier_semaphore()
    for who in peer:
        pl.semaphore_signal(barrier, inc=1, device_id=peer[who], device_id_type=MESH)
    pl.semaphore_wait(barrier, len(peer))

    quarter = pl.ds(pl.multiple_of(x * 96, 96), 96)
    loads[0].wait()
    quart = remote(res.at[0, quarter], res.at[1, quarter], quart_s, quart_r, "across")
    quart.start()
    loads[1].wait()
    swap_par = remote(par.at[0], par.at[1], swap_s.at[0], swap_r.at[0], "sibling")
    swap_par.start()
    loads[2].wait()
    swap_down = remote(down.at[0], down.at[1], swap_s.at[1], swap_r.at[1], "sibling")
    swap_down.start()

    def flip_copy(j):
        return remote(flip.at[j], flip_sib.at[j], flip_s.at[j], flip_r.at[j], "sibling")

    def op_copy(j):
        return remote(
            op_send.at[j], op_recv.at[(j + 3) % 6], op_s.at[j], op_r.at[(j + 3) % 6], "partner"
        )

    def pg_copies(j):
        low = pl.ds(TILE, TILE)
        return [
            remote(pg_send_b.at[j], pg_b.at[j, low], pg_s.at[0, j], pg_r.at[0, j], "sibling"),
            remote(pg_send_a.at[j], pg_a.at[j, low], pg_s.at[1, j], pg_r.at[1, j], "sibling"),
        ]

    def w_copy(side):
        return remote(rest_send, rest_near.at[side], w_s.at[side], w_r.at[side], ways[side])

    def zp_copy(side, j):
        return remote(
            pg_b.at[j], pg_near.at[side, j], zp_s.at[side, j], zp_r.at[side, j], ways[side]
        )

    def chunk(k):
        return pl.ds(pl.multiple_of(k * CHUNK, CHUNK), CHUNK)

    def za_copy(side, k):
        rows = chunk(k)
        return remote(
            fresh_a.at[rows], near_a.at[side, rows], za_s.at[side, k], za_r.at[side, k], ways[side]
        )

    def edge_copies(side, k):
        rows = slice(*EDGE[side][k])
        return [
            remote(
                fresh_a.at[rows],
                near_a.at[side, rows],
                za_s.at[side, k],
                za_r.at[side, k],
                ways[side],
            ),
            remote(
                fresh_b.at[rows],
                near_b.at[side, rows],
                zb_s.at[side, k],
                zb_r.at[side, k],
                ways[side],
            ),
        ]

    def gx_copy(side):
        return remote(
            gap_send.at[1 - side], gap_recv.at[side], gx_s.at[side], gx_r.at[side], ways[side]
        )

    def prepare(seq):
        def one(k, _):
            rows = pl.ds(pl.multiple_of(k * TILE, TILE), TILE)
            values = res[seq, rows, :].astype(jnp.float32)
            center = values - jnp.mean(values, axis=1, keepdims=True)
            spread = jnp.mean(center * center, axis=1, keepdims=True)
            nrm[seq * 3 + k] = (center * lax.rsqrt(spread + 1e-05)).astype(jnp.bfloat16)
            return 0

        lax.fori_loop(0, 3, one, 0)

    def step_ahead(seq):
        for c in range(4):
            cols = slice(c * CHUNK, (c + 1) * CHUNK)
            values = res[seq, :, cols].astype(jnp.float32)
            ahead = values - pltpu.roll(values, 383, 0)
            for k in range(3):
                base[seq * 3 + k, :, cols] = ahead[k * TILE : (k + 1) * TILE]

    def forward_in(j, side):
        rows = nrm[j]
        for c in range(2):
            cols = slice(c * CHUNK, (c + 1) * CHUNK)
            wide = slice(side * 512 + c * CHUNK, side * 512 + (c + 1) * CHUNK)
            v = jnp.dot(rows, par[side, :, cols], preferred_element_type=jnp.float32) * factor
            square = v * v
            tangent = jnp.tanh(coeff * v * (1.0 + 0.044715 * square))
            half = 0.5 * (1.0 + tangent)
            hid[:, wide] = (v * half).astype(jnp.bfloat16)
            slope[j, :, wide] = half + 0.5 * coeff * v * (1.0 - tangent * tangent) * (
                1.0 + 3.0 * 0.044715 * square
            )

    def forward_out(j):
        for c in range(4):
            wide = slice(c * CHUNK, (c + 1) * CHUNK)
            part = jnp.dot(
                hid[:, :512], down[0, :, wide], preferred_element_type=jnp.float32
            ) + jnp.dot(hid[:, 512:], down[1, :, wide], preferred_element_type=jnp.float32)
            base[j, :, wide] += part
            op_send[j, :, wide] = part.astype(jnp.bfloat16)
        op_copy(j).start()

    def forward(j, _):
        forward_in(j, 0)
        forward_in(j, 1)
        forward_out(j)
        return 0

    def turn(j, _):
        flip[j] = nrm[j].T
        flip_copy(j).start()
        return 0

    loads[3].wait()
    heat_root = jnp.sqrt(jnp.full((1, 512), 2.0 * drift_stride * heat[0], jnp.float32))

    def keep(k, _):
        rows = pl.ds(pl.multiple_of(k * TILE, TILE), TILE)
        current = par[0, rows, :].astype(jnp.float32)
        still = current - drift_stride * current + heat_root * noise[rows, :].astype(jnp.float32)
        rest[rows, :] = still
        rest_send[rows, :] = still[:, :SHARE].astype(jnp.bfloat16)
        return 0

    prepare(0)
    step_ahead(0)
    forward_in(0, 0)
    lax.fori_loop(0, 8, keep, 0)
    for side in range(2):
        pl.when(sends[side])(w_copy(side).start)
    swap_par.wait_recv()
    forward_in(0, 1)
    swap_down.wait_recv()
    forward_out(0)
    quart.wait_recv()
    spreads = [
        remote(
            res.at[1, quarter], res.at[1, quarter], spread_s.at[k - 1], spread_r.at[k - 1], f"x{k}"
        )
        for k in (1, 2, 3)
    ]
    for copy in spreads:
        copy.start()
    lax.fori_loop(1, 3, forward, 0)
    lax.fori_loop(0, 3, turn, 0)

    for copy in spreads:
        copy.wait_recv()
    prepare(1)
    step_ahead(1)
    lax.fori_loop(3, 6, forward, 0)
    lax.fori_loop(3, 6, turn, 0)

    def backward(j):
        op_copy((j + 3) % 6).wait_recv()
        keepers = lax.broadcasted_iota(jnp.int32, (TILE, 1), 0) + (j % 3) * TILE < 383
        errors = jnp.where(keepers, base[j] + op_recv[j].astype(jnp.float32), 0.0).astype(
            jnp.bfloat16
        )
        for side in (1, 0):
            grad = lax.dot_general(
                errors, down[side], (((1,), (1,)), ((), ())), preferred_element_type=jnp.float32
            )
            grad = (grad * slope[j, :, side * 512 : side * 512 + 512]).astype(jnp.bfloat16)
            if side == 1:
                pg_send_b[j] = grad[:, :SHARE]
                pg_send_a[j] = grad[:, SHARE:]
                for copy in pg_copies(j):
                    copy.start()
            else:
                pg_b[j, :TILE] = grad[:, :SHARE]
                pg_a[j, :TILE] = grad[:, SHARE:]

    def arrive(j):
        for copy in pg_copies(j):
            copy.wait_recv()
        for side in range(2):
            pl.when(sends[side])(zp_copy(side, j).start)
        flip_copy(j).wait_recv()

    def joined(tiles, rows):
        pieces = []
        for j in tiles:
            pieces += [flip[j, rows, :], flip_sib[j, rows, :]]
        return jnp.concatenate(pieces, axis=1)

    def product(tiles, k):
        right = jnp.concatenate(
            [
                pg_b[tiles[0] : tiles[-1] + 1].reshape(2 * TILE * len(tiles), SHARE),
                pg_a[tiles[0] : tiles[-1] + 1].reshape(2 * TILE * len(tiles), KEEP),
            ],
            axis=1,
        )
        return jnp.dot(joined(tiles, chunk(k)), right, preferred_element_type=jnp.float32)

    def gather_near(tiles, fresh_start):
        for side in range(2):

            @pl.when(mixes[side])
            def _():
                for j in tiles:
                    zp_copy(side, j).wait_recv()

                def one(k, _):
                    right = pg_near[side, tiles[0] : tiles[-1] + 1].reshape(
                        2 * TILE * len(tiles), SHARE
                    )
                    more = jnp.dot(
                        joined(tiles, chunk(k)), right, preferred_element_type=jnp.float32
                    )
                    if fresh_start:
                        acc_near[side, chunk(k), :] = more
                    else:
                        near_b[side, chunk(k), :] = (
                            rest_near[side, chunk(k), :].astype(jnp.float32)
                            - (drift_stride * factor) * (acc_near[side, chunk(k), :] + more)
                        ).astype(jnp.bfloat16)
                    return 0

                if not fresh_start:
                    w_copy(side).wait_recv()
                lax.fori_loop(0, 4, one, 0)

    def first_sum(k, _):
        acc[chunk(k), :] = product((3, 4, 5), k)
        return 0

    def second_sum(k, _):
        acc[chunk(k), :] += product((0, 1), k)
        return 0

    backward(3)
    backward(4)
    arrive(3)
    backward(5)
    arrive(4)
    arrive(5)
    lax.fori_loop(0, 4, first_sum, 0)
    backward(0)
    arrive(0)
    gather_near((3, 4, 5), True)
    backward(1)
    arrive(1)
    lax.fori_loop(0, 4, second_sum, 0)
    backward(2)
    arrive(2)

    for k in range(4):
        rows = chunk((k + turned) % 4)
        total = acc[rows, :] + product((2,), (k + turned) % 4)
        moved = (rest[rows, :] - (drift_stride * factor) * total).astype(jnp.bfloat16)
        fresh_b[rows, :] = moved[:, :SHARE]
        fresh_a[rows, :] = moved[:, SHARE:]
        for side in range(2):
            pl.when(sends[side])(za_copy(side, (k + turned) % 4).start)
            if k != 2:

                @pl.when(jnp.logical_not(sends[side]))
                def _():
                    for copy in edge_copies(side, ((0, 1, 2), (1, 0, 2))[side][k - k // 2]):
                        copy.start()

    gather_near((0, 1, 2), False)

    taken = jnp.full((1, 512), mask[0], jnp.int32) == 1
    mates = jnp.full((1, 512), mate[0], jnp.int32)
    picks = (taken & (mates == rank - 1), taken & (mates == rank + 1))
    gap_sum[...] = jnp.zeros((2, 8, 512), jnp.float32)
    pairs = ((0, SHARE, fresh_b, near_b), (SHARE, 512, fresh_a, near_a))

    def add_gap(side, rows, count):
        for first, last, own_ref, near_ref in pairs:
            gap = own_ref[rows, :].astype(jnp.float32) - near_ref[side, rows, :].astype(
                jnp.float32
            )
            gap_sum[side, :, first:last] += jnp.sum(
                (gap * gap).reshape(count // 8, 8, last - first), axis=0
            )

    for side in range(2):

        @pl.when(jnp.logical_not(mixes[side]))
        def _():
            for piece in (0, 1):
                for copy in edge_copies(side, piece):
                    copy.wait_recv()
                first, last = EDGE[side][piece]
                add_gap(side, slice(first, last), last - first)
            gap_send[side] = gap_sum[side]
            gx_copy(1 - side).start()

    def mix(k, _):
        for side in range(2):

            @pl.when(mixes[side])
            def _():
                za_copy(side, k).wait_recv()
                add_gap(side, chunk(k), CHUNK)

        def choose(sides):
            for first, last, own_ref, near_ref in pairs:
                value = own_ref[chunk(k), :]
                for side in sides:
                    value = jnp.where(
                        picks[side][:, first:last], near_ref[side, chunk(k), :], value
                    )
                out_ref[0, chunk(k), first:last] = value

        pl.when(mixes[0] & mixes[1])(lambda: choose((0, 1)))
        pl.when(jnp.logical_not(mixes[0]))(lambda: choose((1,)))
        pl.when(jnp.logical_not(mixes[1]))(lambda: choose((0,)))
        return 0

    lax.fori_loop(0, 4, mix, 0)

    for side in range(2):

        @pl.when(jnp.logical_not(mixes[side]))
        def _():
            for copy in edge_copies(side, 2):
                copy.wait_recv()
            first, last = EDGE[side][2]
            add_gap(side, slice(first, last), last - first)
            gx_copy(side).wait_recv()
            gap_recv[side] += gap_sum[side]
            gap_ref[0, side : side + 1, :] = jnp.sum(gap_recv[side], axis=0, keepdims=True) * (
                1.0 / 1024.0
            )

        @pl.when(mixes[side])
        def _():
            gap_ref[0, side : side + 1, :] = jnp.sum(gap_sum[side], axis=0, keepdims=True) * (
                1.0 / 1024.0
            )

    quart.wait_send()
    swap_par.wait_send()
    swap_down.wait_send()
    for copy in spreads:
        copy.wait_send()

    def finish(j, _):
        flip_copy(j).wait_send()
        op_copy(j).wait_send()
        for copy in pg_copies(j):
            copy.wait_send()
        for side in range(2):
            pl.when(sends[side])(zp_copy(side, j).wait_send)
        return 0

    lax.fori_loop(0, 6, finish, 0)
    for side in range(2):

        @pl.when(sends[side])
        def _():
            w_copy(side).wait_send()
            for k in range(4):
                za_copy(side, k).wait_send()

        @pl.when(jnp.logical_not(sends[side]))
        def _():
            gx_copy(side).wait_send()
            for piece in range(3):
                for copy in edge_copies(side, piece):
                    copy.wait_send()


def body(residual_flow, params, noise, down, heat, mate, mask):
    any_spec = pl.BlockSpec(memory_space=pl.ANY)
    scalar = pl.BlockSpec(memory_space=pltpu.SMEM)
    vmem = pl.BlockSpec(memory_space=pltpu.VMEM)
    bf16, f32 = jnp.bfloat16, jnp.float32
    dma = pltpu.SemaphoreType.DMA
    return pl.pallas_call(
        kernel,
        out_shape=(
            jax.ShapeDtypeStruct((1, 1024, 512), bf16),
            jax.ShapeDtypeStruct((1, 2, 512), f32),
        ),
        in_specs=[any_spec] * 4 + [scalar] * 3,
        out_specs=(vmem, vmem),
        scratch_shapes=[
            pltpu.VMEM((2, 384, 1024), bf16),
            pltpu.VMEM((2, 1024, 512), bf16),
            pltpu.VMEM((1024, 512), bf16),
            pltpu.VMEM((2, 512, 1024), bf16),
            pltpu.VMEM((6, TILE, 1024), bf16),
            pltpu.VMEM((6, 1024, TILE), bf16),
            pltpu.VMEM((6, 1024, TILE), bf16),
            pltpu.VMEM((6, TILE, 1024), f32),
            pltpu.VMEM((6, TILE, 1024), f32),
            pltpu.VMEM((6, TILE, 1024), bf16),
            pltpu.VMEM((6, TILE, 1024), bf16),
            pltpu.VMEM((TILE, 1024), bf16),
            pltpu.VMEM((6, TILE, SHARE), bf16),
            pltpu.VMEM((6, TILE, KEEP), bf16),
            pltpu.VMEM((6, 2 * TILE, SHARE), bf16),
            pltpu.VMEM((6, 2 * TILE, KEEP), bf16),
            pltpu.VMEM((1024, 512), f32),
            pltpu.VMEM((1024, 512), f32),
            pltpu.VMEM((1024, SHARE), bf16),
            pltpu.VMEM((1024, KEEP), bf16),
            pltpu.VMEM((2, 1024, SHARE), bf16),
            pltpu.VMEM((2, 1024, KEEP), bf16),
            pltpu.VMEM((1024, SHARE), bf16),
            pltpu.VMEM((2, 1024, SHARE), bf16),
            pltpu.VMEM((2, 6, 2 * TILE, SHARE), bf16),
            pltpu.VMEM((2, 1024, SHARE), f32),
            pltpu.VMEM((2, 8, 512), f32),
            pltpu.VMEM((2, 8, 512), f32),
            pltpu.VMEM((2, 8, 512), f32),
            dma((4,)),
            dma((2,)),
            dma((2,)),
            dma(()),
            dma(()),
            dma((3,)),
            dma((3,)),
            dma((6,)),
            dma((6,)),
            dma((6,)),
            dma((6,)),
            dma((2, 6)),
            dma((2, 6)),
            dma((2,)),
            dma((2,)),
            dma((2, 6)),
            dma((2, 6)),
            dma((2, 4)),
            dma((2, 4)),
            dma((2, 4)),
            dma((2, 4)),
            dma((2,)),
            dma((2,)),
        ],
        compiler_params=pltpu.CompilerParams(
            collective_id=0, has_side_effects=True, vmem_limit_bytes=52 << 20
        ),
        name="langevin_step",
    )(
        *(
            pltpu.with_memory_space_constraint(each, pltpu.HBM)
            for each in (residual_flow, params, noise, down)
        ),
        heat,
        mate,
        mask,
    )


def solution(mesh):
    placed = (
        P("dp", None),
        P("rep", None, "dp"),
        P("rep", None, "dp"),
        P("dp", None),
        P("rep"),
        P("rep"),
        P("rep"),
    )
    return jax.shard_map(
        body,
        mesh=mesh,
        in_specs=placed,
        out_specs=(P("rep", None, "dp"), P("rep", None, "dp")),
        check_vma=False,
    )
```
